128 devices in a mesh: row: 4 (over z), col: 4 (over y), layer: 8 (over x, core).
Axes of the slice: x: 4, y: 4, z: 4, core: 2. Of those that a mesh axis runs over, the one named last changes fastest.
Arguments:
- wavefunction: float32 [4096, 4096], P('row', 'col'), may hold values from -0.015625 to 1.515625
- start_block: float32 [4096, 2048], P(('col', 'layer'), 'row'), may hold values from -6 to 6
Outputs:
- basis: float32 [4096, 2048], P(('col', 'layer'), 'row')
The draws below stay inside these ranges and needn't reach their ends.
All inputs are finite; a program needn't handle non-finite values.
Results may differ from the reference program's by a relative error of at most 0.0003.
Values sent between devices are 32-bit elements; how exact they have to be, the bound alone decides.
A program may use at most 128 MiB of HBM per device.

```python
import math
import jax
import jax.numpy as jnp
from jax import lax

M = 4096
K = 2048
ITERS = 1


def draw_wavefunction(key, part):
    first_key, second_key = jax.random.split(jax.random.fold_in(key, 17))
    scales = jnp.exp(jax.random.uniform(first_key, (M,), jnp.float32, 0.0, math.log(1.5)))
    noise = jnp.clip(jax.random.normal(second_key, (M, M), jnp.float32), -4.0, 4.0)
    return jnp.diag(scales) + 0.25 / math.sqrt(M) * noise


def shard_levels(stream_key, extent, shards, smallest, largest):
    gain, own = 1.0, jax.random.fold_in(stream_key, 6)
    for position, shards_of in shards:
        steps = jnp.exp(jax.random.uniform(jax.random.fold_in(own, position), (shards_of,), jnp.float32, smallest / len(shards), largest / len(shards)))
        gain = gain * jnp.repeat(steps, extent[position] // shards_of).reshape([-1 if axis == position else 1 for axis in range(len(extent))])
    return gain


def centred(stream_key, shape, deviation, most, shards=(), dtype=jnp.bfloat16):
    gain = shard_levels(stream_key, shape, shards, -0.22, 0.18) if shards else 1.0
    values = jax.random.normal(stream_key, shape, jnp.float32) * deviation * gain
    return jnp.minimum(jnp.maximum(values, -most), most).astype(dtype)


def setup_inputs(seed: int = 0) -> dict:
    arg_keys = jax.random.split(jax.random.key(seed), 3)
    return {
        "wavefunction": draw_wavefunction(jax.random.fold_in(arg_keys[2], 71), 0),
        "start_block": centred(arg_keys[1], (M, K), 1.0, 6.0, ((0, 32), (1, 4)), jnp.float32),
    }


def reference(wavefunction, start_block):
    density = jnp.dot(wavefunction.astype(jnp.float32), wavefunction.T.astype(jnp.float32), precision=lax.Precision.HIGHEST, preferred_element_type=jnp.float32)
    current = start_block
    for iteration in range(ITERS):
        image_block = jnp.dot(density.astype(jnp.float32), current.astype(jnp.float32), precision=lax.Precision.HIGHEST, preferred_element_type=jnp.float32)
        gram_matrix = jnp.dot(image_block.T.astype(jnp.float32), image_block.astype(jnp.float32), precision=lax.Precision.HIGHEST, preferred_element_type=jnp.float32)
        factor = jnp.linalg.cholesky(gram_matrix)
        current = jax.scipy.linalg.solve_triangular(factor, image_block.T, lower=True).T
    return current * math.sqrt(M)
```

```python
import math

import jax
import jax.numpy as jnp
from jax import lax
from jax.experimental import pallas as pl
from jax.experimental.pallas import tpu as pltpu
from jax.sharding import PartitionSpec as P

f32, bf16 = jnp.float32, jnp.bfloat16
B = 128
H = 256
MESH = pl.DeviceIdType.MESH


def split(x):
    hi = x.astype(bf16)
    return hi, (x - hi.astype(f32)).astype(bf16)


def nt(a, b):
    return lax.dot_general(a, b, (((1,), (1,)), ((), ())), preferred_element_type=f32)


def nn(a, b):
    return lax.dot_general(a, b, (((1,), (0,)), ((), ())), preferred_element_type=f32)


def front_kernel(
    psi_ref, start_ref, g_ref, slab_ref,
    psi, phi, plo, sbuf, shi, slo, tpart, tin, tfull, impart, imin, im, ihi, ilo, gpart, gin,
    load_sem, sa, ra, sb, rb, sc, rc, sd, rd, se, re, sf, rf, sg, rg,
):
    row, col, layer = (lax.axis_index(n) for n in ("row", "col", "layer"))
    load = pltpu.make_async_copy(psi_ref, psi, load_sem)
    load.start()
    for n in range(8):
        step, h = n // 2, n % 2
        to_col, to_layer = lax.rem(col + step, 4), 2 * row + h
        here = (row == col) & (to_col == col) & (to_layer == layer)
        src = start_ref.at[:, h * H : (h + 1) * H]
        dst = sbuf.at[pl.ds(pl.multiple_of(layer * B, B), B), :]

        @pl.when(here)
        def _():
            pltpu.make_async_copy(src, dst, ra.at[layer]).start()

        @pl.when(jnp.logical_not(here))
        def _():
            pltpu.make_async_remote_copy(
                src_ref=src, dst_ref=dst, send_sem=sa.at[n], recv_sem=ra.at[layer],
                device_id=(col, to_col, to_layer), device_id_type=MESH,
            ).start()

    load.wait()

    @pl.loop(0, 8)
    def _(i):
        rows = pl.ds(pl.multiple_of(i * B, B), B)
        hi, lo = split(psi[rows, :])
        phi[rows, :] = hi
        plo[rows, :] = lo

    for n in range(8):
        part = sbuf.at[n * B : (n + 1) * B, :]
        pltpu.make_async_copy(part, part, ra.at[n]).wait()
        for h in range(2):
            hi, lo = split(sbuf[n * B : (n + 1) * B, h * B : (h + 1) * B].T)
            shi[h * B : (h + 1) * B, n * B : (n + 1) * B] = hi
            slo[h * B : (h + 1) * B, n * B : (n + 1) * B] = lo

    @pl.loop(0, 4)
    def _(i):
        cols = pl.ds(pl.multiple_of(i * H, H), H)
        tpart[:, cols] = nn(shi[...], phi[:, cols]) + nn(shi[...], plo[:, cols]) + nn(slo[...], phi[:, cols])

    def band(i, size):
        return pl.ds(pl.multiple_of(i * size, size), size)

    sends = []
    for n in range(1, 4):
        to = lax.rem(row + n, 4)
        sends.append(pltpu.make_async_remote_copy(
            src_ref=tpart.at[band(to, 64), :], dst_ref=tin.at[n - 1], send_sem=sb.at[n - 1], recv_sem=rb.at[n - 1],
            device_id=(to, col, layer), device_id_type=MESH,
        ))
    for s in sends:
        s.start()
    for s in sends:
        s.wait_recv()
    tfull[band(row, 64), :] = (tpart[band(row, 64), :] + tin[0]) + (tin[1] + tin[2])
    gathers = []
    for n in range(1, 4):
        to = lax.rem(row + n, 4)
        gathers.append(pltpu.make_async_remote_copy(
            src_ref=tfull.at[band(row, 64), :], dst_ref=tfull.at[band(row, 64), :],
            send_sem=sc.at[n - 1], recv_sem=rc.at[n - 1], device_id=(to, col, layer), device_id_type=MESH,
        ))
    for s in gathers:
        s.start()
    for n in range(1, 4):
        other = tfull.at[band(lax.rem(row + 4 - n, 4), 64), :]
        pltpu.make_async_copy(other, other, rc.at[n - 1]).wait()
    for s in sends + gathers:
        s.wait_send()
    for n in range(4):
        hi, lo = split(tfull[:, n * H : (n + 1) * H])
        shi[:, n * H : (n + 1) * H] = hi
        slo[:, n * H : (n + 1) * H] = lo

    @pl.loop(0, 4)
    def _(i):
        rows = band(i, H)
        impart[:, rows] = nt(shi[...], phi[rows, :]) + nt(shi[...], plo[rows, :]) + nt(slo[...], phi[rows, :])

    sends = []
    for n in range(1, 4):
        to = lax.rem(col + n, 4)
        sends.append(pltpu.make_async_remote_copy(
            src_ref=impart.at[:, band(to, H)], dst_ref=imin.at[n - 1], send_sem=sd.at[n - 1], recv_sem=rd.at[n - 1],
            device_id=(row, to, layer), device_id_type=MESH,
        ))
    for s in sends:
        s.start()
    for s in sends:
        s.wait_recv()
    mine = band(layer, H)
    im[mine, :] = (impart[:, band(col, H)] + imin[0]) + (imin[1] + imin[2])
    for s in sends:
        s.wait_send()
    gathers = []
    for n in range(1, 8):
        to = lax.rem(layer + n, 8)
        gathers.append(pltpu.make_async_remote_copy(
            src_ref=im.at[mine, :], dst_ref=im.at[mine, :], send_sem=se.at[n - 1], recv_sem=re.at[n - 1],
            device_id=(row, col, to), device_id_type=MESH,
        ))
    for s in gathers:
        s.start()
    for n in range(1, 8):
        other = im.at[band(lax.rem(layer + 8 - n, 8), H), :]
        pltpu.make_async_copy(other, other, re.at[n - 1]).wait()
    for s in gathers:
        s.wait_send()
    half = lax.rem(layer, 2)
    to_row, to_layer = lax.div(layer, 2), 2 * col + half
    stays = (to_row == row) & (row == col) & (to_layer == layer)
    mine = im.at[:, band(half, B)]

    @pl.when(stays)
    def _():
        pltpu.make_async_copy(mine, slab_ref, rg).start()

    @pl.when(jnp.logical_not(stays))
    def _():
        pltpu.make_async_remote_copy(
            src_ref=mine, dst_ref=slab_ref, send_sem=sg, recv_sem=rg,
            device_id=(to_row, row, to_layer), device_id_type=MESH,
        ).start()

    @pl.loop(0, 8)
    def _(i):
        rows = band(i, H)
        hi, lo = split(im[rows, :])
        ihi[rows, :] = hi
        ilo[rows, :] = lo

    @pl.loop(0, 17)
    def _(t):
        first = t <= layer
        i = band(jnp.where(first, layer, 15 - layer), B)
        j = band(jnp.where(first, t, t - layer - 1), B)
        gpart[:, band(t, B)] = nt(ihi[i, :], ihi[j, :]) + nt(ihi[i, :], ilo[j, :]) + nt(ilo[i, :], ihi[j, :])

    group = 4 * row + col
    sends = []
    for n in range(1, 16):
        to = lax.rem(group + n, 16)
        sends.append(pltpu.make_async_remote_copy(
            src_ref=gpart.at[band(to, 8), :], dst_ref=gin.at[n - 1], send_sem=sf.at[n - 1], recv_sem=rf.at[n - 1],
            device_id=(lax.div(to, 4), lax.rem(to, 4), layer), device_id_type=MESH,
        ))
    for s in sends:
        s.start()
    total = gpart[band(group, 8), :]
    for n, s in enumerate(sends):
        s.wait_recv()
        total = total + gin[n]
    g_ref[...] = total
    for s in sends:
        s.wait_send()
    pltpu.make_async_copy(slab_ref, slab_ref, rg).wait()

    @pl.when(jnp.logical_not(stays))
    def _():
        pltpu.make_async_copy(mine, mine, sg).wait()

    for n in range(8):
        step, h = n // 2, n % 2
        to_col, to_layer = lax.rem(col + step, 4), 2 * row + h
        here = (row == col) & (to_col == col) & (to_layer == layer)

        @pl.when(jnp.logical_not(here))
        def _():
            src = start_ref.at[:, h * H : (h + 1) * H]
            pltpu.make_async_copy(src, src, sa.at[n]).wait()


def front(wavefunction, start_block):
    dma = pltpu.SemaphoreType.DMA
    return pl.pallas_call(
        front_kernel,
        out_shape=(jax.ShapeDtypeStruct((8, 17 * B), f32), jax.ShapeDtypeStruct((2048, B), f32)),
        in_specs=[pl.BlockSpec(memory_space=pl.ANY)] * 2,
        out_specs=[pl.BlockSpec(memory_space=pltpu.VMEM)] * 2,
        scratch_shapes=[
            pltpu.VMEM((1024, 1024), f32), pltpu.VMEM((1024, 1024), bf16), pltpu.VMEM((1024, 1024), bf16),
            pltpu.VMEM((1024, H), f32), pltpu.VMEM((H, 1024), bf16), pltpu.VMEM((H, 1024), bf16),
            pltpu.VMEM((H, 1024), f32), pltpu.VMEM((3, 64, 1024), f32), pltpu.VMEM((H, 1024), f32),
            pltpu.VMEM((H, 1024), f32), pltpu.VMEM((3, H, H), f32),
            pltpu.VMEM((2048, H), f32), pltpu.VMEM((2048, H), bf16), pltpu.VMEM((2048, H), bf16),
            pltpu.VMEM((B, 17 * B), f32), pltpu.VMEM((15, 8, 17 * B), f32),
            dma, dma((8,)), dma((8,)), dma((3,)), dma((3,)), dma((3,)), dma((3,)), dma((3,)), dma((3,)),
            dma((7,)), dma((7,)), dma((15,)), dma((15,)), dma, dma,
        ],
        compiler_params=pltpu.CompilerParams(has_side_effects=True, vmem_limit_bytes=48 * 1024 * 1024),
    )(wavefunction, start_block)


def factor(d_ref, y_ref):
    lane = lax.broadcasted_iota(jnp.int32, (8, B), 1)
    sub = lax.broadcasted_iota(jnp.int32, (8, B), 0)
    full = lambda x: jnp.broadcast_to(x, (8, B))
    state = [d_ref[8 * i : 8 * i + 8, :] for i in range(16)]
    for b in range(16):
        cols = [[full(state[i][:, 8 * b + j : 8 * b + j + 1]) for j in range(8)] for i in range(b, 16)]
        c = list(cols[0])
        inside = (lane >= 8 * b) & (lane < 8 * b + 8)
        v = jnp.where(inside, jnp.where(lane - 8 * b == sub, 1.0, 0.0), state[b])
        out = jnp.zeros((8, B), f32)
        for j in range(8):
            pivot = full(c[j][j : j + 1, :])
            r = 1.0 / pivot
            f = c[j] * r
            vj = full(v[j : j + 1, :])
            out = jnp.where(sub == j, vj * lax.rsqrt(pivot), out)
            v = jnp.where(sub == j, vj * r, v - f * vj)
            for k in range(j + 1, 8):
                t = full(c[k][j : j + 1, :])
                c[k] = jnp.where(sub == j, t * r, c[k] - f * t)
        y_ref[8 * b : 8 * b + 8, :] = jnp.where(lane <= 8 * b + sub, out, 0.0)
        w = [full(v[j : j + 1, :]) for j in range(8)]
        for i in range(b + 1, 16):
            p = [cols[i - b][j] * w[j] for j in range(8)]
            q = ((p[0] + p[1]) + (p[2] + p[3])) + ((p[4] + p[5]) + (p[6] + p[7]))
            state[i] = jnp.where(inside, 0.0, state[i]) - q


def solve_kernel(scale, g_ref, s_ref, q_ref, w, la, lb, yb, d, y, qs, st, sems):
    copies = []
    for l in range(8):
        n = (l + 1) * B
        copies.append(pltpu.make_async_copy(g_ref.at[l, :, 0:n], w.at[l * B : (l + 1) * B, 0:n], sems.at[2 * l]))
        copies.append(pltpu.make_async_copy(
            g_ref.at[l, :, n : 17 * B], w.at[(15 - l) * B : (16 - l) * B, 0 : 17 * B - n], sems.at[2 * l + 1]
        ))
    copies.append(pltpu.make_async_copy(s_ref, st, sems.at[16]))
    for c in copies:
        c.start()
    slab = slice(16 * B, 17 * B)
    copies[16].wait()
    for n in range(16):
        w[slab, n * B : (n + 1) * B] = st[n * B : (n + 1) * B, :].T
    for c in copies[:16]:
        c.wait()

    def store(rows, x, half):
        hi, lo = split(x)
        for n, (a, b) in enumerate(((hi, hi), (hi, lo), (lo, hi))):
            at = slice((3 * half + n) * B, (3 * half + n + 1) * B)
            la[rows, at] = a
            lb[rows, at] = b

    def triple(x):
        hi, lo = split(x)
        return jnp.concatenate([hi, hi, lo], 1)

    def invert(c):
        d[...] = w[c, c]
        factor(d, y)
        hi, lo = split(y[...])
        yb[...] = jnp.concatenate([hi, lo, hi], 1)

    @pl.loop(0, 8)
    def _(K):
        c0 = pl.ds(pl.multiple_of(K * H, H), B)
        c1 = pl.ds(pl.multiple_of(K * H + B, B), B)
        near = slice(0, 3 * B)
        invert(c0)

        def panel(rows):
            p = nt(triple(w[rows, c0]), yb[...])
            store(rows, p, 0)
            w[rows, c1] -= nt(la[rows, near], lb[c1, near])
            return p

        panel(c1)

        @pl.loop(K + 1, 8)
        def _(I):
            panel(pl.ds(pl.multiple_of(I * H, H), H))

        qs[:, c0] = panel(slab)
        invert(c1)

        @pl.loop(K + 1, 8)
        def _(I):
            rows = pl.ds(pl.multiple_of(I * H, H), H)
            store(rows, nt(triple(w[rows, c1]), yb[...]), 1)

        p = nt(triple(w[slab, c1]), yb[...])
        store(slab, p, 1)
        qs[:, c1] = p

        @pl.loop(K + 1, 8)
        def _(J):
            cj = pl.ds(pl.multiple_of(J * H, H), H)
            w[slab, cj] -= nt(la[slab, :], lb[cj, :])

            @pl.loop(J, 8)
            def _(I):
                ci = pl.ds(pl.multiple_of(I * H, H), H)
                w[ci, cj] -= nt(la[ci, :], lb[cj, :])

    q_ref[...] = qs[:, pl.ds(pl.multiple_of(lax.axis_index("row") * 512, 512), 512)] * scale


def solve(gram, slab, scale):
    return pl.pallas_call(
        lambda *refs: solve_kernel(scale, *refs),
        out_shape=jax.ShapeDtypeStruct((B, 512), f32),
        in_specs=[pl.BlockSpec(memory_space=pl.ANY)] * 2,
        out_specs=pl.BlockSpec(memory_space=pltpu.VMEM),
        scratch_shapes=[
            pltpu.VMEM((17 * B, 2048), f32), pltpu.VMEM((17 * B, 6 * B), bf16), pltpu.VMEM((17 * B, 6 * B), bf16),
            pltpu.VMEM((B, 3 * B), bf16), pltpu.VMEM((B, B), f32), pltpu.VMEM((B, B), f32),
            pltpu.VMEM((B, 2048), f32), pltpu.VMEM((2048, B), f32), pltpu.SemaphoreType.DMA((17,)),
        ],
        compiler_params=pltpu.CompilerParams(vmem_limit_bytes=60 * 1024 * 1024),
    )(gram, slab)


def shards(wavefunction, start_block):
    piece, slab = front(wavefunction, start_block)
    gram = lax.all_gather(piece, ("row", "col", "layer"), axis=0)
    gram = gram.reshape(16, 8, 8, 17 * B).transpose(1, 0, 2, 3).reshape(8, B, 17 * B)
    return solve(gram, slab, math.sqrt(4096.0))


def solution(mesh):
    placed = (P("row", "col"), P(("col", "layer"), "row"))
    return jax.shard_map(
        shards, mesh=mesh, in_specs=placed, out_specs=P(("col", "layer"), "row"), check_vma=False
    )
```

```python
import math

import jax
import jax.numpy as jnp
from jax import lax
from jax.experimental import pallas as pl
from jax.experimental.pallas import tpu as pltpu
from jax.sharding import PartitionSpec as P

f32, bf16 = jnp.float32, jnp.bfloat16
B = 128
H = 256
MESH = pl.DeviceIdType.MESH


def split(x):
    hi = x.astype(bf16)
    return hi, (x - hi.astype(f32)).astype(bf16)


def nt(a, b):
    return lax.dot_general(a, b, (((1,), (1,)), ((), ())), preferred_element_type=f32)


def nn(a, b):
    return lax.dot_general(a, b, (((1,), (0,)), ((), ())), preferred_element_type=f32)


def band(i, size):
    return pl.ds(pl.multiple_of(i * size, size), size)


def done(ref, sem):
    pltpu.make_async_copy(ref, ref, sem).wait()


def greet(devices):
    barrier = pltpu.get_barrier_semaphore()
    for d in devices:
        pl.semaphore_signal(barrier, inc=1, device_id=d, device_id_type=MESH)
    pl.semaphore_wait(barrier, len(devices))


def send(src, dst, send_sem, recv_sem, device):
    copy = pltpu.make_async_remote_copy(
        src_ref=src, dst_ref=dst, send_sem=send_sem, recv_sem=recv_sem, device_id=device, device_id_type=MESH
    )
    copy.start()
    return copy


def front_kernel(
    psi, start, all_ref, slab_ref,
    phi, plo, tile, bands, planes, st, shi, slo, tpart, tin, tfull, impart, imin, im, ihi, ilo, gpart, gin, turned, g_ref,
    s1, r1, s2, r2, s3, r3, sb, rb, sc, rc, sd, rd, se, re, sp, rp, sf, rf, own_sem, sh, rh, si, ri, sj, rj,
):
    row, col, layer = (lax.axis_index(n) for n in ("row", "col", "layer"))
    group = 4 * row + col
    plane = [lax.rem(group + n, 16) for n in range(1, 16)]
    plane = [(lax.div(p, 4), lax.rem(p, 4), layer) for p in plane]
    greet(plane + [(row, col, lax.rem(layer + n, 8)) for n in range(1, 8)])
    for n in range(4):
        tile[n * B : (n + 1) * B, :] = start[:, n * B : (n + 1) * B].T
    pieces = []
    for n in range(1, 8):
        to = lax.rem(layer + n, 8)
        pieces.append(send(tile.at[band(to, 64), :], bands.at[:, band(layer, B)], s1.at[n - 1], r1.at[n - 1], (row, col, to)))
    bands[:, band(layer, B)] = tile[band(layer, 64), :]

    @pl.loop(0, 8)
    def _(i):
        rows = band(i, B)
        hi, lo = split(psi[rows, :])
        phi[rows, :] = hi
        plo[rows, :] = lo

    for n in range(1, 8):
        done(bands.at[:, band(lax.rem(layer + 8 - n, 8), B)], r1.at[n - 1])
    for n in range(1, 4):
        to = lax.rem(col + n, 4)
        pieces.append(send(bands, planes.at[n - 1], s2.at[n - 1], r2.at[n - 1], (row, to, layer)))

    def pass_on(n, src):
        to = lax.rem(col + 4 - n, 4)

        @pl.when(to == row)
        def _():
            st[band(row, 64), :] = src[...]

        @pl.when(to != row)
        def _():
            send(src, st.at[band(row, 64), :], s3.at[n], r3.at[lax.rem(to + 4 - row, 4) - 1], (to, col, layer))

    pass_on(0, bands)
    for n in range(1, 4):
        done(planes.at[n - 1], r2.at[n - 1])
        pass_on(n, planes.at[n - 1])
    for n in range(1, 4):
        done(st.at[band(lax.rem(row + 4 - n, 4), 64), :], r3.at[n - 1])
    hi, lo = split(st[...])
    shi[...] = hi
    slo[...] = lo

    @pl.loop(0, 4)
    def _(i):
        cols = band(i, H)
        tpart[:, cols] = nn(shi[...], phi[:, cols]) + nn(shi[...], plo[:, cols]) + nn(slo[...], phi[:, cols])

    sums = []
    for n in range(1, 4):
        to = lax.rem(row + n, 4)
        sums.append(send(tpart.at[band(to, 64), :], tin.at[n - 1], sb.at[n - 1], rb.at[n - 1], (to, col, layer)))
    for s in sums:
        s.wait_recv()
    tfull[band(row, 64), :] = (tpart[band(row, 64), :] + tin[0]) + (tin[1] + tin[2])
    for n in range(1, 4):
        to = lax.rem(row + n, 4)
        mine = tfull.at[band(row, 64), :]
        pieces.append(send(mine, mine, sc.at[n - 1], rc.at[n - 1], (to, col, layer)))
    for n in range(1, 4):
        done(tfull.at[band(lax.rem(row + 4 - n, 4), 64), :], rc.at[n - 1])
    hi, lo = split(tfull[...])
    shi[...] = hi
    slo[...] = lo

    @pl.loop(0, 8)
    def _(i):
        rows = band(i, B)
        impart[i] = nt(phi[rows, :], shi[...]) + nt(plo[rows, :], shi[...]) + nt(phi[rows, :], slo[...])

    part = []
    for n in range(1, 4):
        to = lax.rem(col + n, 4)
        part.append(send(impart.at[:, band(to, 32), :], imin.at[n - 1], sd.at[n - 1], rd.at[n - 1], (row, to, layer)))
    for s in part:
        s.wait_recv()
    own = (impart[:, band(col, 32), :] + imin[0]) + (imin[1] + imin[2])
    im[:, layer] = own.reshape(H, H).T.reshape(4, 64, H)
    other = (row, col, layer + 1 - 2 * lax.rem(layer, 2))
    mine = im.at[:, layer]
    for n in range(1, 4):
        to = lax.rem(layer + 2 * n, 8)
        pieces.append(send(mine, mine, se.at[n - 1], re.at[n - 1], (row, col, to)))
    pieces.append(send(mine, mine, sp.at[0], rp.at[0], other))
    for n in range(1, 4):
        came = im.at[:, lax.rem(layer + 8 - 2 * n, 8)]
        done(came, re.at[n - 1])
        pieces.append(send(came, came, sp.at[n], rp.at[n], other))
    for n in range(4):
        done(im.at[:, lax.rem(other[2] + 8 - 2 * n, 8)], rp.at[n])
    for n in range(4):
        rows = slice(n * 512, (n + 1) * 512)
        hi, lo = split(im[n].reshape(512, H))
        ihi[rows, :] = hi
        ilo[rows, :] = lo

    @pl.loop(0, 17)
    def _(t):
        first = t <= layer
        i = band(jnp.where(first, layer, 15 - layer), B)
        j = band(jnp.where(first, t, t - layer - 1), B)
        gpart[:, band(t, B)] = nt(ihi[i, :], ihi[j, :]) + nt(ihi[i, :], ilo[j, :]) + nt(ilo[i, :], ihi[j, :])

    grams = []
    for n in range(1, 16):
        to = lax.rem(group + n, 16)
        grams.append(send(gpart.at[band(to, 8), :], gin.at[n - 1], sf.at[n - 1], rf.at[n - 1], plane[n - 1]))
    lanes = band(lax.div(layer, 4), B)
    for n in range(16):
        turned[...] = im[n // 4, 2 * (n % 4) : 2 * (n % 4) + 2, :, lanes].reshape(B, B).T
        slab_ref[:, n * B : (n + 1) * B] = turned[band(lax.rem(layer, 4), 32), :]
    total = gpart[band(group, 8), :]
    for n, s in enumerate(grams):
        s.wait_recv()
        total = total + gin[n]
    g_ref[...] = total
    x, core = lax.div(layer, 2), lax.rem(layer, 2)
    at = {"z": row, "y": col, "x": x}
    spots = []

    def device(place):
        return (place["z"], place["y"], 2 * place["x"] + core)

    def away(axis, n):
        return {**at, axis: lax.rem(at[axis] + n + 4, 4)}

    def cells(place, lanes, k=core, along=None):
        index = [slice(None) if a == along else place[a] for a in "zyx"]
        return all_ref.at[index[0], index[1], index[2], k, :, lanes]

    parts = [("xyz", slice(0, 6 * B)), ("yzx", slice(6 * B, 12 * B)), ("zxy", slice(12 * B, 17 * B))]
    keep = pltpu.make_async_copy(g_ref, all_ref.at[row, col, x, core], own_sem)
    keep.start()
    for c, (order, lanes) in enumerate(parts):
        for n in range(1, 4):
            pieces.append(send(g_ref.at[:, lanes], cells(at, lanes), sh.at[c, n - 1], rh.at[c, n - 1], device(away(order[0], n))))
    keep.wait()

    def line(c, place):
        order, lanes = parts[c]
        return cells(place, lanes, along=order[0])

    def share(c, place, slot):
        order, lanes = parts[c]
        src = cells(place, lanes, along=order[0])
        pieces.append(send(src, src, sj.at[c, slot], rj.at[c, slot], (row, col, layer + 1 - 2 * core)))

    def outward(c, place, j, directions):
        src = line(c, place)
        for d in directions:
            slot = 3 + j + (0 if d == 1 else 6)
            pieces.append(send(src, src, si.at[c, slot], ri.at[c, slot], device(away(parts[c][0][2], d))))

    for c, (order, lanes) in enumerate(parts):
        for n in range(1, 4):
            done(cells(away(order[0], -n), lanes), rh.at[c, n - 1])
        for n in range(1, 4):
            pieces.append(send(line(c, at), line(c, at), si.at[c, n - 1], ri.at[c, n - 1], device(away(order[1], n))))
        outward(c, at, 0, (1, -1))
        share(c, at, 0)
    for n in range(1, 4):
        for c, (order, lanes) in enumerate(parts):
            place = away(order[1], -n)
            done(line(c, place), ri.at[c, n - 1])
            outward(c, place, n, (1, -1))
            share(c, place, n)
    for n in range(4):
        for c, (order, lanes) in enumerate(parts):
            for d in (1, -1):
                place = {**away(order[1], -n), order[2]: lax.rem(at[order[2]] - d + 4, 4)}
                done(line(c, place), ri.at[c, 3 + n + (0 if d == 1 else 6)])
                if (n < 2) == (d == 1):
                    src = line(c, place)
                    slot = 3 + 4 + n % 2 + (0 if d == 1 else 6)
                    pieces.append(send(src, src, si.at[c, slot], ri.at[c, slot], device(away(order[2], d))))
                share(c, place, 4 + n + (0 if d == 1 else 4))
    for n in range(4):
        for c, (order, lanes) in enumerate(parts):
            d = 1 if n < 2 else -1
            place = {**away(order[1], -n), order[2]: lax.rem(at[order[2]] + 2, 4)}
            done(line(c, place), ri.at[c, 3 + 4 + n % 2 + (0 if d == 1 else 6)])
            share(c, place, 12 + n)
    for slot in range(16):
        for c, (order, lanes) in enumerate(parts):
            n = slot % 4
            place = away(order[1], -n)
            shift = (0, -1, 1, 2)[slot // 4]
            place = {**place, order[2]: lax.rem(at[order[2]] + shift + 4, 4)}
            done(cells(place, lanes, 1 - core, order[0]), rj.at[c, slot])
    for s in pieces + sums + part + grams:
        s.wait_send()
    for n in range(4):

        @pl.when(lax.rem(col + 4 - n, 4) != row)
        def _():
            done(bands, s3.at[n])


def front(wavefunction, start_block):
    dma = pltpu.SemaphoreType.DMA
    vmem = pltpu.VMEM
    return pl.pallas_call(
        front_kernel,
        out_shape=(jax.ShapeDtypeStruct((4, 4, 4, 2, 8, 17 * B), f32), jax.ShapeDtypeStruct((32, 2048), f32)),
        in_specs=[pl.BlockSpec(memory_space=pltpu.VMEM)] * 2,
        out_specs=[pl.BlockSpec(memory_space=pl.ANY), pl.BlockSpec(memory_space=pltpu.VMEM)],
        scratch_shapes=[
            vmem((1024, 1024), bf16), vmem((1024, 1024), bf16), vmem((512, B), f32), vmem((64, 1024), f32),
            vmem((3, 64, 1024), f32), vmem((H, 1024), f32), vmem((H, 1024), bf16), vmem((H, 1024), bf16),
            vmem((H, 1024), f32), vmem((3, 64, 1024), f32), vmem((H, 1024), f32),
            vmem((8, B, H), f32), vmem((3, 8, 32, H), f32),
            vmem((4, 8, 64, H), f32), vmem((2048, H), bf16), vmem((2048, H), bf16),
            vmem((B, 17 * B), f32), vmem((15, 8, 17 * B), f32), vmem((B, B), f32), vmem((8, 17 * B), f32),
            dma((7,)), dma((7,)), dma((3,)), dma((3,)), dma((4,)), dma((3,)), dma((3,)), dma((3,)), dma((3,)), dma((3,)),
            dma((3,)), dma((3,)), dma((3,)), dma((3,)), dma((4,)), dma((4,)), dma((15,)), dma((15,)),
            dma, dma((3, 3)), dma((3, 3)), dma((3, 15)), dma((3, 15)), dma((3, 16)), dma((3, 16)),
        ],
        compiler_params=pltpu.CompilerParams(
            collective_id=0, has_side_effects=True, vmem_limit_bytes=48 * 1024 * 1024
        ),
    )(wavefunction, start_block)


def back_kernel(scale, q_ref, out_ref, buf, send_sem, recv_sem):
    row, col, layer = (lax.axis_index(n) for n in ("row", "col", "layer"))
    group = 4 * row + col
    plane = [lax.rem(group + n, 16) for n in range(1, 16)]
    greet([(lax.div(p, 4), lax.rem(p, 4), layer) for p in plane])
    for n in range(4):
        src = q_ref.at[:, n * 512 : (n + 1) * 512]

        @pl.when((n == row) & (row == col))
        def _():
            buf[col] = src[...]

        @pl.when((n != row) | (row != col))
        def _():
            send(src, buf.at[col], send_sem.at[n], recv_sem.at[col], (n, row, layer))

    for n in range(4):

        @pl.when((n != col) | (row != col))
        def _():
            done(buf.at[n], recv_sem.at[n])

        out_ref[n * 32 : (n + 1) * 32, :] = buf[n] * scale
    for n in range(4):

        @pl.when((n != row) | (row != col))
        def _():
            done(buf.at[n], send_sem.at[n])


def back(q, scale):
    dma = pltpu.SemaphoreType.DMA
    return pl.pallas_call(
        lambda *refs: back_kernel(scale, *refs),
        out_shape=jax.ShapeDtypeStruct((B, 512), f32),
        in_specs=[pl.BlockSpec(memory_space=pltpu.VMEM)],
        out_specs=pl.BlockSpec(memory_space=pltpu.VMEM),
        scratch_shapes=[pltpu.VMEM((4, 32, 512), f32), dma((4,)), dma((4,))],
        compiler_params=pltpu.CompilerParams(collective_id=1, has_side_effects=True),
    )(q)


def factor(d_ref, y_ref):
    lane = lax.broadcasted_iota(jnp.int32, (8, B), 1)
    sub = lax.broadcasted_iota(jnp.int32, (8, B), 0)
    full = lambda x: jnp.broadcast_to(x, (8, B))
    state = [d_ref[8 * i : 8 * i + 8, :] for i in range(16)]
    for b in range(16):
        cols = [[full(state[i][:, 8 * b + j : 8 * b + j + 1]) for j in range(8)] for i in range(b, 16)]
        c = list(cols[0])
        inside = (lane >= 8 * b) & (lane < 8 * b + 8)
        v = jnp.where(inside, jnp.where(lane - 8 * b == sub, 1.0, 0.0), state[b])
        out = jnp.zeros((8, B), f32)
        for j in range(8):
            pivot = full(c[j][j : j + 1, :])
            r = 1.0 / pivot
            f = c[j] * r
            vj = full(v[j : j + 1, :])
            out = jnp.where(sub == j, vj * lax.rsqrt(pivot), out)
            v = jnp.where(sub == j, vj * r, v - f * vj)
            for k in range(j + 1, 8):
                t = full(c[k][j : j + 1, :])
                c[k] = jnp.where(sub == j, t * r, c[k] - f * t)
        y_ref[8 * b : 8 * b + 8, :] = jnp.where(lane <= 8 * b + sub, out, 0.0)
        w = [full(v[j : j + 1, :]) for j in range(8)]
        for i in range(b + 1, 16):
            p = [cols[i - b][j] * w[j] for j in range(8)]
            q = ((p[0] + p[1]) + (p[2] + p[3])) + ((p[4] + p[5]) + (p[6] + p[7]))
            state[i] = jnp.where(inside, 0.0, state[i]) - q


def solve_kernel(g_ref, s_ref, q_ref, w, la, lb, yb, d, y, sems):
    sizes = [((l + 1) * B, (16 - l) * B) for l in range(8)]

    @pl.loop(0, 16)
    def _(q):
        for l, (n, m) in enumerate(sizes):
            rows = pl.ds(pl.multiple_of(l * B + q * 8, 8), 8)
            pltpu.make_async_copy(g_ref.at[q, l, :, 0:n], w.at[rows, 0:n], sems.at[2 * l]).start()
            rows = pl.ds(pl.multiple_of((15 - l) * B + q * 8, 8), 8)
            pltpu.make_async_copy(g_ref.at[q, l, :, n : 17 * B], w.at[rows, 0:m], sems.at[2 * l + 1]).start()

    slab = slice(16 * B, 16 * B + 32)
    w[slab, :] = s_ref[...]
    for l, (n, m) in enumerate(sizes):
        done(w.at[l * B : (l + 1) * B, 0:n], sems.at[2 * l])
        done(w.at[(15 - l) * B : (16 - l) * B, 0:m], sems.at[2 * l + 1])

    def store(rows, x, half):
        hi, lo = split(x)
        for n, (a, b) in enumerate(((hi, hi), (hi, lo), (lo, hi))):
            at = slice((3 * half + n) * B, (3 * half + n + 1) * B)
            la[rows, at] = a
            lb[rows, at] = b

    def triple(x):
        hi, lo = split(x)
        return jnp.concatenate([hi, hi, lo], 1)

    def invert(c):
        d[...] = w[c, c]
        factor(d, y)
        hi, lo = split(y[...])
        yb[...] = jnp.concatenate([hi, lo, hi], 1)

    @pl.loop(0, 8)
    def _(K):
        c0 = pl.ds(pl.multiple_of(K * H, H), B)
        c1 = pl.ds(pl.multiple_of(K * H + B, B), B)
        near = slice(0, 3 * B)
        invert(c0)

        def panel(rows):
            p = nt(triple(w[rows, c0]), yb[...])
            store(rows, p, 0)
            w[rows, c1] -= nt(la[rows, near], lb[c1, near])
            return p

        panel(c1)

        @pl.loop(K + 1, 8)
        def _(I):
            panel(pl.ds(pl.multiple_of(I * H, H), H))

        q_ref[:, c0] = panel(slab)
        invert(c1)

        @pl.loop(K + 1, 8)
        def _(I):
            rows = pl.ds(pl.multiple_of(I * H, H), H)
            store(rows, nt(triple(w[rows, c1]), yb[...]), 1)

        p = nt(triple(w[slab, c1]), yb[...])
        store(slab, p, 1)
        q_ref[:, c1] = p

        @pl.loop(K + 1, 8)
        def _(J):
            cj = pl.ds(pl.multiple_of(J * H, H), H)
            w[slab, cj] -= nt(la[slab, :], lb[cj, :])

            @pl.loop(J, 8)
            def _(I):
                ci = pl.ds(pl.multiple_of(I * H, H), H)
                w[ci, cj] -= nt(la[ci, :], lb[cj, :])


def solve(gram, slab):
    return pl.pallas_call(
        solve_kernel,
        out_shape=jax.ShapeDtypeStruct((32, 2048), f32),
        in_specs=[pl.BlockSpec(memory_space=pl.ANY), pl.BlockSpec(memory_space=pltpu.VMEM)],
        out_specs=pl.BlockSpec(memory_space=pltpu.VMEM),
        scratch_shapes=[
            pltpu.VMEM((16 * B + 32, 2048), f32), pltpu.VMEM((16 * B + 32, 6 * B), bf16),
            pltpu.VMEM((16 * B + 32, 6 * B), bf16),
            pltpu.VMEM((B, 3 * B), bf16), pltpu.VMEM((B, B), f32), pltpu.VMEM((B, B), f32), pltpu.SemaphoreType.DMA((16,)),
        ],
        compiler_params=pltpu.CompilerParams(vmem_limit_bytes=60 * 1024 * 1024),
    )(gram, slab)


def shards(wavefunction, start_block):
    gram, slab = front(wavefunction, start_block)
    gram = gram.reshape(16, 8, 8, 17 * B)
    return back(solve(gram, slab), math.sqrt(4096.0))


def solution(mesh):
    placed = (P("row", "col"), P(("col", "layer"), "row"))
    return jax.shard_map(
        shards, mesh=mesh, in_specs=placed, out_specs=P(("col", "layer"), "row"), check_vma=False
    )
```

```python
import math

import jax
import jax.numpy as jnp
from jax import lax
from jax.experimental import pallas as pl
from jax.experimental.pallas import tpu as pltpu
from jax.sharding import PartitionSpec as P

f32, bf16 = jnp.float32, jnp.bfloat16
B = 128
H = 256
MESH = pl.DeviceIdType.MESH


def split(x):
    hi = x.astype(bf16)
    return hi, (x - hi.astype(f32)).astype(bf16)


def nt(a, b):
    return lax.dot_general(a, b, (((1,), (1,)), ((), ())), preferred_element_type=f32)


def nn(a, b):
    return lax.dot_general(a, b, (((1,), (0,)), ((), ())), preferred_element_type=f32)


def band(i, size):
    return pl.ds(pl.multiple_of(i * size, size), size)


def done(ref, sem):
    pltpu.make_async_copy(ref, ref, sem).wait()


def greet(devices):
    barrier = pltpu.get_barrier_semaphore()
    for d in devices:
        pl.semaphore_signal(barrier, inc=1, device_id=d, device_id_type=MESH)
    pl.semaphore_wait(barrier, len(devices))


def send(src, dst, send_sem, recv_sem, device):
    copy = pltpu.make_async_remote_copy(
        src_ref=src, dst_ref=dst, send_sem=send_sem, recv_sem=recv_sem, device_id=device, device_id_type=MESH
    )
    copy.start()
    return copy


def front_kernel(
    psi_ref, start_ref, all_ref, slab_ref,
    psi, start,
    phi, plo, tile, bands, planes, st, shi, slo, tpart, tin, tfull, impart, imin, im, ihi, ilo, gpart, gin, turned, g_ref,
    s1, r1, s2, r2, s3, r3, sb, rb, sc, rc, sd, rd, se, re, sp, rp, sf, rf, own_sem, load_sem, sh, rh, si, ri, sj, rj,
):
    row, col, layer = (lax.axis_index(n) for n in ("row", "col", "layer"))
    group = 4 * row + col
    plane = [lax.rem(group + n, 16) for n in range(1, 16)]
    plane = [(lax.div(p, 4), lax.rem(p, 4), layer) for p in plane]
    loads = [pltpu.make_async_copy(start_ref, start, load_sem.at[0]), pltpu.make_async_copy(psi_ref, psi, load_sem.at[1])]
    for c in loads:
        c.start()
    greet(plane + [(row, col, lax.rem(layer + n, 8)) for n in range(1, 8)])
    loads[0].wait()
    for n in range(4):
        tile[n * B : (n + 1) * B, :] = start[:, n * B : (n + 1) * B].T
    pieces = []
    for n in range(1, 8):
        to = lax.rem(layer + n, 8)
        pieces.append(send(tile.at[band(to, 64), :], bands.at[:, band(layer, B)], s1.at[n - 1], r1.at[n - 1], (row, col, to)))
    bands[:, band(layer, B)] = tile[band(layer, 64), :]

    loads[1].wait()

    @pl.loop(0, 8)
    def _(i):
        rows = band(i, B)
        hi, lo = split(psi[rows, :])
        phi[rows, :] = hi
        plo[rows, :] = lo

    for n in range(1, 8):
        done(bands.at[:, band(lax.rem(layer + 8 - n, 8), B)], r1.at[n - 1])
    for n in range(1, 4):
        to = lax.rem(col + n, 4)
        pieces.append(send(bands, planes.at[n - 1], s2.at[n - 1], r2.at[n - 1], (row, to, layer)))

    def pass_on(n, src):
        to = lax.rem(col + 4 - n, 4)

        @pl.when(to == row)
        def _():
            st[band(row, 64), :] = src[...]

        @pl.when(to != row)
        def _():
            send(src, st.at[band(row, 64), :], s3.at[n], r3.at[lax.rem(to + 4 - row, 4) - 1], (to, col, layer))

    pass_on(0, bands)
    for n in range(1, 4):
        done(planes.at[n - 1], r2.at[n - 1])
        pass_on(n, planes.at[n - 1])
    for n in range(1, 4):
        done(st.at[band(lax.rem(row + 4 - n, 4), 64), :], r3.at[n - 1])
    hi, lo = split(st[...])
    shi[...] = hi
    slo[...] = lo

    @pl.loop(0, 4)
    def _(i):
        cols = band(i, H)
        tpart[:, cols] = nn(shi[...], phi[:, cols]) + nn(shi[...], plo[:, cols]) + nn(slo[...], phi[:, cols])

    sums = []
    for n in range(1, 4):
        to = lax.rem(row + n, 4)
        sums.append(send(tpart.at[band(to, 64), :], tin.at[n - 1], sb.at[n - 1], rb.at[n - 1], (to, col, layer)))
    for s in sums:
        s.wait_recv()
    tfull[band(row, 64), :] = (tpart[band(row, 64), :] + tin[0]) + (tin[1] + tin[2])
    for n in range(1, 4):
        to = lax.rem(row + n, 4)
        mine = tfull.at[band(row, 64), :]
        pieces.append(send(mine, mine, sc.at[n - 1], rc.at[n - 1], (to, col, layer)))
    for n in range(1, 4):
        done(tfull.at[band(lax.rem(row + 4 - n, 4), 64), :], rc.at[n - 1])
    hi, lo = split(tfull[...])
    shi[...] = hi
    slo[...] = lo

    @pl.loop(0, 8)
    def _(i):
        rows = band(i, B)
        impart[i] = nt(phi[rows, :], shi[...]) + nt(plo[rows, :], shi[...]) + nt(phi[rows, :], slo[...])

    part = []
    for n in range(1, 4):
        to = lax.rem(col + n, 4)
        part.append(send(impart.at[:, band(to, 32), :], imin.at[n - 1], sd.at[n - 1], rd.at[n - 1], (row, to, layer)))
    for s in part:
        s.wait_recv()
    own = (impart[:, band(col, 32), :] + imin[0]) + (imin[1] + imin[2])
    im[:, layer] = own.reshape(H, H).T.reshape(4, 64, H)
    other = (row, col, layer + 1 - 2 * lax.rem(layer, 2))
    mine = im.at[:, layer]
    for n in range(1, 4):
        to = lax.rem(layer + 2 * n, 8)
        pieces.append(send(mine, mine, se.at[n - 1], re.at[n - 1], (row, col, to)))
    pieces.append(send(mine, mine, sp.at[0], rp.at[0], other))
    for n in range(1, 4):
        came = im.at[:, lax.rem(layer + 8 - 2 * n, 8)]
        done(came, re.at[n - 1])
        pieces.append(send(came, came, sp.at[n], rp.at[n], other))
    for n in range(4):
        done(im.at[:, lax.rem(other[2] + 8 - 2 * n, 8)], rp.at[n])
    for n in range(4):
        rows = slice(n * 512, (n + 1) * 512)
        hi, lo = split(im[n].reshape(512, H))
        ihi[rows, :] = hi
        ilo[rows, :] = lo

    @pl.loop(0, 17)
    def _(t):
        first = t <= layer
        i = band(jnp.where(first, layer, 15 - layer), B)
        j = band(jnp.where(first, t, t - layer - 1), B)
        gpart[:, band(t, B)] = nt(ihi[i, :], ihi[j, :]) + nt(ihi[i, :], ilo[j, :]) + nt(ilo[i, :], ihi[j, :])

    grams = []
    for n in range(1, 16):
        to = lax.rem(group + n, 16)
        grams.append(send(gpart.at[band(to, 8), :], gin.at[n - 1], sf.at[n - 1], rf.at[n - 1], plane[n - 1]))
    lanes = band(lax.div(layer, 4), B)
    for n in range(16):
        turned[...] = im[n // 4, 2 * (n % 4) : 2 * (n % 4) + 2, :, lanes].reshape(B, B).T
        slab_ref[:, n * B : (n + 1) * B] = turned[band(lax.rem(layer, 4), 32), :]
    total = gpart[band(group, 8), :]
    for n, s in enumerate(grams):
        s.wait_recv()
        total = total + gin[n]
    g_ref[...] = total
    x, core = lax.div(layer, 2), lax.rem(layer, 2)
    at = {"z": row, "y": col, "x": x}
    spots = []

    def device(place):
        return (place["z"], place["y"], 2 * place["x"] + core)

    def away(axis, n):
        return {**at, axis: lax.rem(at[axis] + n + 4, 4)}

    def cells(place, lanes, k=core, along=None):
        index = [slice(None) if a == along else place[a] for a in "zyx"]
        return all_ref.at[index[0], index[1], index[2], k, :, lanes]

    parts = [("xyz", slice(0, 6 * B)), ("yzx", slice(6 * B, 12 * B)), ("zxy", slice(12 * B, 17 * B))]
    keep = pltpu.make_async_copy(g_ref, all_ref.at[row, col, x, core], own_sem)
    keep.start()
    for c, (order, lanes) in enumerate(parts):
        for n in range(1, 4):
            pieces.append(send(g_ref.at[:, lanes], cells(at, lanes), sh.at[c, n - 1], rh.at[c, n - 1], device(away(order[0], n))))
    keep.wait()

    def line(c, place):
        order, lanes = parts[c]
        return cells(place, lanes, along=order[0])

    def share(c, place, slot):
        order, lanes = parts[c]
        src = cells(place, lanes, along=order[0])
        pieces.append(send(src, src, sj.at[c, slot], rj.at[c, slot], (row, col, layer + 1 - 2 * core)))

    def outward(c, place, j, directions):
        src = line(c, place)
        for d in directions:
            slot = 3 + j + (0 if d == 1 else 6)
            pieces.append(send(src, src, si.at[c, slot], ri.at[c, slot], device(away(parts[c][0][2], d))))

    for c, (order, lanes) in enumerate(parts):
        for n in range(1, 4):
            done(cells(away(order[0], -n), lanes), rh.at[c, n - 1])
        for n in range(1, 4):
            pieces.append(send(line(c, at), line(c, at), si.at[c, n - 1], ri.at[c, n - 1], device(away(order[1], n))))
        outward(c, at, 0, (1, -1))
        share(c, at, 0)
    for n in range(1, 4):
        for c, (order, lanes) in enumerate(parts):
            place = away(order[1], -n)
            done(line(c, place), ri.at[c, n - 1])
            outward(c, place, n, (1, -1))
            share(c, place, n)
    for n in range(4):
        for c, (order, lanes) in enumerate(parts):
            for d in (1, -1):
                place = {**away(order[1], -n), order[2]: lax.rem(at[order[2]] - d + 4, 4)}
                done(line(c, place), ri.at[c, 3 + n + (0 if d == 1 else 6)])
                if (n < 2) == (d == 1):
                    src = line(c, place)
                    slot = 3 + 4 + n % 2 + (0 if d == 1 else 6)
                    pieces.append(send(src, src, si.at[c, slot], ri.at[c, slot], device(away(order[2], d))))
                share(c, place, 4 + n + (0 if d == 1 else 4))
    for n in range(4):
        for c, (order, lanes) in enumerate(parts):
            d = 1 if n < 2 else -1
            place = {**away(order[1], -n), order[2]: lax.rem(at[order[2]] + 2, 4)}
            done(line(c, place), ri.at[c, 3 + 4 + n % 2 + (0 if d == 1 else 6)])
            share(c, place, 12 + n)
    for slot in range(16):
        for c, (order, lanes) in enumerate(parts):
            n = slot % 4
            place = away(order[1], -n)
            shift = (0, -1, 1, 2)[slot // 4]
            place = {**place, order[2]: lax.rem(at[order[2]] + shift + 4, 4)}
            done(cells(place, lanes, 1 - core, order[0]), rj.at[c, slot])
    for s in pieces + sums + part + grams:
        s.wait_send()
    for n in range(4):

        @pl.when(lax.rem(col + 4 - n, 4) != row)
        def _():
            done(bands, s3.at[n])


def front(wavefunction, start_block):
    dma = pltpu.SemaphoreType.DMA
    vmem = pltpu.VMEM
    return pl.pallas_call(
        front_kernel,
        out_shape=(jax.ShapeDtypeStruct((4, 4, 4, 2, 8, 17 * B), f32), jax.ShapeDtypeStruct((32, 2048), f32)),
        in_specs=[pl.BlockSpec(memory_space=pl.ANY)] * 2,
        out_specs=[pl.BlockSpec(memory_space=pl.ANY), pl.BlockSpec(memory_space=pltpu.VMEM)],
        scratch_shapes=[
            vmem((1024, 1024), f32), vmem((B, 512), f32), vmem((1024, 1024), bf16), vmem((1024, 1024), bf16), vmem((512, B), f32), vmem((64, 1024), f32),
            vmem((3, 64, 1024), f32), vmem((H, 1024), f32), vmem((H, 1024), bf16), vmem((H, 1024), bf16),
            vmem((H, 1024), f32), vmem((3, 64, 1024), f32), vmem((H, 1024), f32),
            vmem((8, B, H), f32), vmem((3, 8, 32, H), f32),
            vmem((4, 8, 64, H), f32), vmem((2048, H), bf16), vmem((2048, H), bf16),
            vmem((B, 17 * B), f32), vmem((15, 8, 17 * B), f32), vmem((B, B), f32), vmem((8, 17 * B), f32),
            dma((7,)), dma((7,)), dma((3,)), dma((3,)), dma((4,)), dma((3,)), dma((3,)), dma((3,)), dma((3,)), dma((3,)),
            dma((3,)), dma((3,)), dma((3,)), dma((3,)), dma((4,)), dma((4,)), dma((15,)), dma((15,)),
            dma, dma((2,)), dma((3, 3)), dma((3, 3)), dma((3, 15)), dma((3, 15)), dma((3, 16)), dma((3, 16)),
        ],
        compiler_params=pltpu.CompilerParams(
            collective_id=0, has_side_effects=True, vmem_limit_bytes=63 * 1024 * 1024
        ),
    )(wavefunction, start_block)


def back_kernel(scale, q_ref, out_ref, mid, buf, s1, r1, s2, r2):
    row, col, layer = (lax.axis_index(n) for n in ("row", "col", "layer"))
    turns = [(lax.rem(row + n, 4), lax.rem(row + 4 - n, 4)) for n in range(1, 4)]
    sides = [(lax.rem(col + n, 4), lax.rem(col + 4 - n, 4)) for n in range(1, 4)]
    greet([(to, col, layer) for to, _ in turns] + [(row, to, layer) for to, _ in sides])
    sends = []
    for n, (to, _) in enumerate(turns):
        sends.append(send(q_ref.at[:, band(to, 512)], mid.at[n], s1.at[n], r1.at[n], (to, col, layer)))

    def pass_on(n, src, to):
        @pl.when(to == col)
        def _():
            buf[col] = src[...]

        @pl.when(to != col)
        def _():
            send(src, buf.at[col], s2.at[n], r2.at[lax.rem(to + 4 - col, 4) - 1], (row, to, layer))

    pass_on(0, q_ref.at[:, band(row, 512)], row)
    for n, (_, source) in enumerate(turns):
        done(mid.at[n], r1.at[n])
        pass_on(n + 1, mid.at[n], source)
    for n, (_, source) in enumerate(sides):
        done(buf.at[source], r2.at[n])
    for n in range(4):
        out_ref[n * 32 : (n + 1) * 32, :] = buf[n] * scale
    for s in sends:
        s.wait_send()
    for n, to in enumerate([row] + [source for _, source in turns]):

        @pl.when(to != col)
        def _():
            done(buf.at[0], s2.at[n])


def back(q, scale):
    dma = pltpu.SemaphoreType.DMA
    return pl.pallas_call(
        lambda *refs: back_kernel(scale, *refs),
        out_shape=jax.ShapeDtypeStruct((B, 512), f32),
        in_specs=[pl.BlockSpec(memory_space=pltpu.VMEM)],
        out_specs=pl.BlockSpec(memory_space=pltpu.VMEM),
        scratch_shapes=[
            pltpu.VMEM((3, 32, 512), f32), pltpu.VMEM((4, 32, 512), f32), dma((3,)), dma((3,)), dma((4,)), dma((3,)),
        ],
        compiler_params=pltpu.CompilerParams(collective_id=1, has_side_effects=True),
    )(q)


def factor(d_ref, y_ref, fill):
    lane = lax.broadcasted_iota(jnp.int32, (8, B), 1)
    sub = lax.broadcasted_iota(jnp.int32, (8, B), 0)
    full = lambda x: jnp.broadcast_to(x, (8, B))
    state = [d_ref[8 * i : 8 * i + 8, :] for i in range(16)]
    for b in range(16):
        turned = [[full(state[i][:, 8 * b + j : 8 * b + j + 1]) for i in range(b, 16)] for j in range(8)]
        c = [jnp.where(sub < 8, turned[j][0], 0.0) for j in range(8)]
        inside = (lane >= 8 * b) & (lane < 8 * b + 8)
        v = jnp.where(inside, jnp.where(lane - 8 * b == sub, 1.0, 0.0), state[b])
        out, pivots, inverse = v, c[0], 1.0
        for j in range(8):
            q = 1.0 / c[j]
            r = full(q[j : j + 1, :])
            if j:
                out = jnp.where(sub >= j, v, out)
                pivots = jnp.where(sub >= j, c[j], pivots)
            inverse = jnp.where(sub >= j, q, inverse)
            f = jnp.where(sub == j, 0.0, c[j] * r)
            v = v - f * full(v[j : j + 1, :])
            for k in range(j + 1, 8):
                c[k] = c[k] - f * full(c[k][j : j + 1, :])
        y_ref[8 * b : 8 * b + 8, :] = jnp.where(lane <= 8 * b + sub, out * lax.rsqrt(pivots), 0.0)
        v = v * inverse
        w = [full(v[j : j + 1, :]) for j in range(8)]
        for i in range(b + 1, 16):
            p = [turned[j][i - b] * w[j] for j in range(8)]
            q = ((p[0] + p[1]) + (p[2] + p[3])) + ((p[4] + p[5]) + (p[6] + p[7]))
            state[i] = jnp.where(inside, 0.0, state[i]) - q
        fill(b)


def solve_kernel(g_ref, s_ref, q_ref, w, lhi, llo, yhi, ylo, d, y, sems):
    sizes = [((l + 1) * B, (16 - l) * B) for l in range(8)]

    @pl.loop(0, 16)
    def _(q):
        for l, (n, m) in enumerate(sizes):
            rows = pl.ds(pl.multiple_of(l * B + q * 8, 8), 8)
            pltpu.make_async_copy(g_ref.at[q, l, :, 0:n], w.at[rows, 0:n], sems.at[2 * l]).start()
            rows = pl.ds(pl.multiple_of((15 - l) * B + q * 8, 8), 8)
            pltpu.make_async_copy(g_ref.at[q, l, :, n : 17 * B], w.at[rows, 0:m], sems.at[2 * l + 1]).start()

    slab = slice(16 * B, 16 * B + 32)
    w[slab, :] = s_ref[...]
    w[0:B, 7 * H : 8 * H] = jnp.zeros((B, H), f32)

    @pl.loop(0, 10)
    def _(i):
        lhi[band(i, H), :] = jnp.zeros((H, H), bf16)
        llo[band(i, H), :] = jnp.zeros((H, H), bf16)

    yhi[0:B, B:H] = jnp.zeros((B, B), bf16)
    ylo[0:B, B:H] = jnp.zeros((B, B), bf16)
    for l, (n, m) in enumerate(sizes):
        done(w.at[l * B : (l + 1) * B, 0:n], sems.at[2 * l])
        done(w.at[(15 - l) * B : (16 - l) * B, 0:m], sems.at[2 * l + 1])

    def nt3(a, b):
        (ahi, alo), (bhi, blo) = a, b
        return nt(ahi, bhi) + nt(ahi, blo) + nt(alo, bhi)

    def nn3(a, b):
        (ahi, alo), (bhi, blo) = a, b
        return nn(ahi, bhi) + nn(ahi, blo) + nn(alo, bhi)

    def keep(rows, x):
        lhi[rows, :], llo[rows, :] = split(x)

    def held(rows):
        return lhi[rows, :], llo[rows, :]

    def panel(rows, cols):
        p = nt3(split(w[rows, cols]), (yhi[...], ylo[...]))
        keep(rows, p)
        return p

    def tile(I, J, source, size=H):
        rows, cols = band(I, size), band(J, H)
        w[rows, cols] -= nt3(held(band(source, size)), held(cols))

    @pl.loop(0, 8)
    def _(K):
        c0 = pl.ds(pl.multiple_of(K * H, H), B)
        c1 = pl.ds(pl.multiple_of(K * H + B, B), B)
        both = band(K, H)
        side = 7 - K
        total = side * (side + 1)

        def half(t):
            tri, pair = lax.div(t, 2), lax.rem(t, 2)
            n = jnp.int32(0)
            for step in range(1, 7):
                n = n + jnp.where(tri >= step * (step + 1) // 2, 1, 0)
            J = 7 - n
            I = 7 - (tri - lax.div(n * (n + 1), 2))
            real = (t < total) & (K > 0)
            tile(jnp.where(real, 2 * I + pair, 0), jnp.where(real, J, 7), jnp.where(real, 2 * I + pair, 18), B)

        d[...] = w[c0, c0]
        factor(d, y, lambda b: half(b))
        first = split(y[...])
        yhi[0:B, 0:B], ylo[0:B, 0:B] = first
        l21 = split(nt3(split(w[c1, c0]), first))
        d[...] = w[c1, c1] - nt3(l21, l21)
        corner = split(nn3(l21, first))
        factor(d, y, lambda b: half(16 + b))
        second = split(y[...])
        yhi[B:H, B:H], ylo[B:H, B:H] = second
        yhi[B:H, 0:B], ylo[B:H, 0:B] = split(-nn3(second, corner))

        @pl.when(K > 0)
        def _():
            @pl.loop(16, jnp.maximum(lax.div(total, 2), 16))
            def _(t):
                half(2 * t)
                half(2 * t + 1)

            @pl.loop(K, 8)
            def _(J):
                cols = band(J, H)
                w[slab, cols] -= nt3(held(slab), held(cols))

        q_ref[:, both] = panel(slab, both)

        @pl.loop(K + 1, 8)
        def _(I):
            panel(band(I, H), both)

        @pl.when(K < 7)
        def _():
            cols = band(K + 1, H)

            @pl.loop(K + 1, 8)
            def _(I):
                w[band(I, H), cols] -= nt3(held(band(I, H)), held(cols))


def solve(gram, slab):
    return pl.pallas_call(
        solve_kernel,
        out_shape=jax.ShapeDtypeStruct((32, 2048), f32),
        in_specs=[pl.BlockSpec(memory_space=pl.ANY), pl.BlockSpec(memory_space=pltpu.VMEM)],
        out_specs=pl.BlockSpec(memory_space=pltpu.VMEM),
        scratch_shapes=[
            pltpu.VMEM((16 * B + 32, 2048), f32), pltpu.VMEM((2560, H), bf16), pltpu.VMEM((2560, H), bf16),
            pltpu.VMEM((H, H), bf16), pltpu.VMEM((H, H), bf16),
            pltpu.VMEM((B, B), f32), pltpu.VMEM((B, B), f32), pltpu.SemaphoreType.DMA((16,)),
        ],
        compiler_params=pltpu.CompilerParams(vmem_limit_bytes=60 * 1024 * 1024),
    )(gram, slab)


def shards(wavefunction, start_block):
    gram, slab = front(wavefunction, start_block)
    gram = gram.reshape(16, 8, 8, 17 * B)
    return back(solve(gram, slab), math.sqrt(4096.0))


def solution(mesh):
    placed = (P("row", "col"), P(("col", "layer"), "row"))
    return jax.shard_map(
        shards, mesh=mesh, in_specs=placed, out_specs=P(("col", "layer"), "row"), check_vma=False
    )
```

```python
import math

import jax
import jax.numpy as jnp
from jax import lax
from jax.experimental import pallas as pl
from jax.experimental.pallas import tpu as pltpu
from jax.sharding import PartitionSpec as P

f32, bf16 = jnp.float32, jnp.bfloat16
B = 128
H = 256
MESH = pl.DeviceIdType.MESH


def split(x):
    hi = x.astype(bf16)
    return hi, (x - hi.astype(f32)).astype(bf16)


def nt(a, b):
    return lax.dot_general(a, b, (((1,), (1,)), ((), ())), preferred_element_type=f32)


def nn(a, b):
    return lax.dot_general(a, b, (((1,), (0,)), ((), ())), preferred_element_type=f32)


def band(i, size):
    return pl.ds(pl.multiple_of(i * size, size), size)


def done(ref, sem):
    pltpu.make_async_copy(ref, ref, sem).wait()


def greet(devices):
    barrier = pltpu.get_barrier_semaphore()
    for d in devices:
        pl.semaphore_signal(barrier, inc=1, device_id=d, device_id_type=MESH)
    pl.semaphore_wait(barrier, len(devices))


def send(src, dst, send_sem, recv_sem, device):
    copy = pltpu.make_async_remote_copy(
        src_ref=src, dst_ref=dst, send_sem=send_sem, recv_sem=recv_sem, device_id=device, device_id_type=MESH
    )
    copy.start()
    return copy


def front_kernel(
    psi_ref, start_ref, all_ref, slab_ref,
    psi, start,
    phi, plo, tile, bands, planes, st, shi, slo, tpart, tin, tfull, impart, imin, im, ihi, ilo, gpart, gin, turned, g_ref,
    s1, r1, s2, r2, s3, r3, sb, rb, sc, rc, sd, rd, se, re, sp, rp, sf, rf, own_sem, load_sem, sh, rh, si, ri, sj, rj,
):
    row, col, layer = (lax.axis_index(n) for n in ("row", "col", "layer"))
    group = 4 * row + col
    plane = [lax.rem(group + n, 16) for n in range(1, 16)]
    plane = [(lax.div(p, 4), lax.rem(p, 4), layer) for p in plane]
    loads = [pltpu.make_async_copy(start_ref, start, load_sem.at[0]), pltpu.make_async_copy(psi_ref, psi, load_sem.at[1])]
    for c in loads:
        c.start()
    greet(plane + [(row, col, lax.rem(layer + n, 8)) for n in range(1, 8)])
    loads[0].wait()
    for n in range(4):
        tile[n * B : (n + 1) * B, :] = start[:, n * B : (n + 1) * B].T
    pieces = []
    for n in range(1, 8):
        to = lax.rem(layer + n, 8)
        pieces.append(send(tile.at[band(to, 64), :], bands.at[:, band(layer, B)], s1.at[n - 1], r1.at[n - 1], (row, col, to)))
    bands[:, band(layer, B)] = tile[band(layer, 64), :]

    loads[1].wait()

    @pl.loop(0, 8)
    def _(i):
        rows = band(i, B)
        hi, lo = split(psi[rows, :])
        phi[rows, :] = hi
        plo[rows, :] = lo

    for n in range(1, 8):
        done(bands.at[:, band(lax.rem(layer + 8 - n, 8), B)], r1.at[n - 1])
    halves = [slice(h * 32, (h + 1) * 32) for h in range(2)]
    ups = [lax.rem(row + n, 4) for n in range(4)]
    downs = [lax.rem(row + 4 - n, 4) for n in range(4)]
    for h, part in enumerate(halves):
        for n in range(1, 4):
            to = lax.rem(col + n, 4)
            pieces.append(send(bands.at[part, :], planes.at[n - 1, part, :], s2.at[h, n - 1], r2.at[h, n - 1], (row, to, layer)))

    def pass_on(h, n, src):
        to = lax.rem(col + 4 - n, 4)
        dst = st.at[h, band(row, 32), :]

        @pl.when(to == row)
        def _():
            st[h, band(row, 32), :] = src[...]

        @pl.when(to != row)
        def _():
            send(src, dst, s3.at[h, n], r3.at[h, lax.rem(to + 4 - row, 4) - 1], (to, col, layer))

    for h, part in enumerate(halves):
        pass_on(h, 0, bands.at[part, :])
        for n in range(1, 4):
            done(planes.at[n - 1, part, :], r2.at[h, n - 1])
            pass_on(h, n, planes.at[n - 1, part, :])
    for h in range(2):
        for n in range(1, 4):
            done(st.at[h, band(downs[n], 32), :], r3.at[h, n - 1])
        hi, lo = split(st[h])
        shi[h] = hi
        slo[h] = lo

        @pl.loop(0, 4)
        def _(i):
            cols = band(i, H)
            tpart[h, :, cols] = nn(shi[h], phi[:, cols]) + nn(shi[h], plo[:, cols]) + nn(slo[h], phi[:, cols])

        for n in range(1, 4):
            pieces.append(send(
                tpart.at[h, band(ups[n], 32), :], tin.at[h, n - 1], sb.at[h, n - 1], rb.at[h, n - 1], (ups[n], col, layer)
            ))
    for h in range(2):
        for n in range(3):
            done(tin.at[h, n], rb.at[h, n])
        mine = band(row, 32)
        tfull[h, mine, :] = (tpart[h, mine, :] + tin[h, 0]) + (tin[h, 1] + tin[h, 2])
        for n in (1, 3):
            mine = tfull.at[h, band(row, 32), :]
            pieces.append(send(mine, mine, sc.at[h, n - 1], rc.at[h, n - 1], (ups[n], col, layer)))
    for h in range(2):
        for n, skip in ((1, 0), (3, 16)):
            done(tfull.at[h, band(downs[n], 32), :], rc.at[h, n - 1])
            near = tfull.at[h, pl.ds(pl.multiple_of(downs[n] * 32 + skip, 16), 16), :]
            slot = 1 if n == 1 else 3
            pieces.append(send(near, near, sc.at[h, slot], rc.at[h, slot], (ups[n], col, layer)))
    for h in range(2):
        for slot, skip in ((1, 0), (3, 16)):
            done(tfull.at[h, pl.ds(pl.multiple_of(ups[2] * 32 + skip, 16), 16), :], rc.at[h, slot])
        hi, lo = split(tfull[h])
        shi[h] = hi
        slo[h] = lo

        @pl.loop(0, 4)
        def _(i):
            rows = band(i, H)
            p = nt(phi[rows, :], shi[h]) + nt(plo[rows, :], shi[h]) + nt(phi[rows, :], slo[h])
            impart[h, pl.ds(2 * i, 2)] = p.reshape(2, B, B)

        for n in range(1, 4):
            to = lax.rem(col + n, 4)
            pieces.append(send(
                impart.at[h, :, band(to, 32), :], imin.at[h, n - 1], sd.at[h, n - 1], rd.at[h, n - 1], (row, to, layer)
            ))
    other = (row, col, layer + 1 - 2 * lax.rem(layer, 2))
    for h, part in enumerate(halves):
        for n in range(3):
            done(imin.at[h, n], rd.at[h, n])
        own = (impart[h, :, band(col, 32), :] + imin[h, 0]) + (imin[h, 1] + imin[h, 2])
        im[:, layer, part] = own.reshape(H, B).T.reshape(4, 32, H)
        mine = im.at[:, layer, part]
        for n in range(1, 4):
            to = lax.rem(layer + 2 * n, 8)
            pieces.append(send(mine, mine, se.at[h, n - 1], re.at[h, n - 1], (row, col, to)))
        pieces.append(send(mine, mine, sp.at[h, 0], rp.at[h, 0], other))
    for h, part in enumerate(halves):
        for n in (1, 3, 2):
            came = im.at[:, lax.rem(layer + 8 - 2 * n, 8), part]
            done(came, re.at[h, n - 1])
            pieces.append(send(came, came, sp.at[h, n], rp.at[h, n], other))
    for h, part in enumerate(halves):
        for n in range(4):
            done(im.at[:, lax.rem(other[2] + 8 - 2 * n, 8), part], rp.at[h, n])
    for n in range(4):
        rows = slice(n * 512, (n + 1) * 512)
        hi, lo = split(im[n].reshape(512, H))
        ihi[rows, :] = hi
        ilo[rows, :] = lo

    @pl.loop(0, 17)
    def _(t):
        first = t <= layer
        i = band(jnp.where(first, layer, 15 - layer), B)
        j = band(jnp.where(first, t, t - layer - 1), B)
        gpart[:, band(t, B)] = nt(ihi[i, :], ihi[j, :]) + nt(ihi[i, :], ilo[j, :]) + nt(ilo[i, :], ihi[j, :])

    parts = [("xyz", slice(0, 6 * B)), ("yzx", slice(6 * B, 12 * B)), ("zxy", slice(12 * B, 17 * B))]
    grams = []
    for c, (order, lanes) in enumerate(parts):
        for n in range(1, 16):
            to = lax.rem(group + n, 16)
            grams.append(send(
                gpart.at[band(to, 8), lanes], gin.at[n - 1, :, lanes], sf.at[c, n - 1], rf.at[c, n - 1], plane[n - 1]
            ))
    lanes = band(lax.div(layer, 4), B)
    for n in range(16):
        turned[...] = im[n // 4, 2 * (n % 4) : 2 * (n % 4) + 2, :, lanes].reshape(B, B).T
        slab_ref[:, n * B : (n + 1) * B] = turned[band(lax.rem(layer, 4), 32), :]
    x, core = lax.div(layer, 2), lax.rem(layer, 2)
    at = {"z": row, "y": col, "x": x}
    spots = []

    def device(place):
        return (place["z"], place["y"], 2 * place["x"] + core)

    def away(axis, n):
        return {**at, axis: lax.rem(at[axis] + n + 4, 4)}

    def cells(place, lanes, k=core, along=None):
        index = [slice(None) if a == along else place[a] for a in "zyx"]
        return all_ref.at[index[0], index[1], index[2], k, :, lanes]

    for c, (order, lanes) in enumerate(parts):
        total = gpart[band(group, 8), lanes]
        for n in range(1, 16):
            done(gin.at[n - 1, :, lanes], rf.at[c, n - 1])
            total = total + gin[n - 1, :, lanes]
        g_ref[:, lanes] = total
        pltpu.make_async_copy(g_ref.at[:, lanes], cells(at, lanes), own_sem.at[c]).start()
        for n in range(1, 4):
            pieces.append(send(g_ref.at[:, lanes], cells(at, lanes), sh.at[c, n - 1], rh.at[c, n - 1], device(away(order[0], n))))

    def line(c, place):
        order, lanes = parts[c]
        return cells(place, lanes, along=order[0])

    def share(c, place, slot):
        order, lanes = parts[c]
        src = cells(place, lanes, along=order[0])
        pieces.append(send(src, src, sj.at[c, slot], rj.at[c, slot], (row, col, layer + 1 - 2 * core)))

    def outward(c, place, j, directions):
        src = line(c, place)
        for d in directions:
            slot = 3 + j + (0 if d == 1 else 6)
            pieces.append(send(src, src, si.at[c, slot], ri.at[c, slot], device(away(parts[c][0][2], d))))

    for c, (order, lanes) in enumerate(parts):
        for n in range(1, 4):
            done(cells(away(order[0], -n), lanes), rh.at[c, n - 1])
        done(g_ref.at[:, lanes], own_sem.at[c])
        for n in range(1, 4):
            pieces.append(send(line(c, at), line(c, at), si.at[c, n - 1], ri.at[c, n - 1], device(away(order[1], n))))
        outward(c, at, 0, (1, -1))
        share(c, at, 0)
    for n in range(1, 4):
        for c, (order, lanes) in enumerate(parts):
            place = away(order[1], -n)
            done(line(c, place), ri.at[c, n - 1])
            outward(c, place, n, (1, -1))
            share(c, place, n)
    for n in range(4):
        for c, (order, lanes) in enumerate(parts):
            for d in (1, -1):
                place = {**away(order[1], -n), order[2]: lax.rem(at[order[2]] - d + 4, 4)}
                done(line(c, place), ri.at[c, 3 + n + (0 if d == 1 else 6)])
                if (n < 2) == (d == 1):
                    src = line(c, place)
                    slot = 3 + 4 + n % 2 + (0 if d == 1 else 6)
                    pieces.append(send(src, src, si.at[c, slot], ri.at[c, slot], device(away(order[2], d))))
                share(c, place, 4 + n + (0 if d == 1 else 4))
    for n in range(4):
        for c, (order, lanes) in enumerate(parts):
            d = 1 if n < 2 else -1
            place = {**away(order[1], -n), order[2]: lax.rem(at[order[2]] + 2, 4)}
            done(line(c, place), ri.at[c, 3 + 4 + n % 2 + (0 if d == 1 else 6)])
            share(c, place, 12 + n)
    for slot in range(16):
        for c, (order, lanes) in enumerate(parts):
            n = slot % 4
            place = away(order[1], -n)
            shift = (0, -1, 1, 2)[slot // 4]
            place = {**place, order[2]: lax.rem(at[order[2]] + shift + 4, 4)}
            done(cells(place, lanes, 1 - core, order[0]), rj.at[c, slot])
    for s in pieces + grams:
        s.wait_send()
    for h, part in enumerate(halves):
        for n in range(4):

            @pl.when(lax.rem(col + 4 - n, 4) != row)
            def _():
                done(bands.at[part, :], s3.at[h, n])


def front(wavefunction, start_block):
    dma = pltpu.SemaphoreType.DMA
    vmem = pltpu.VMEM
    return pl.pallas_call(
        front_kernel,
        out_shape=(jax.ShapeDtypeStruct((4, 4, 4, 2, 8, 17 * B), f32), jax.ShapeDtypeStruct((32, 2048), f32)),
        in_specs=[pl.BlockSpec(memory_space=pl.ANY)] * 2,
        out_specs=[pl.BlockSpec(memory_space=pl.ANY), pl.BlockSpec(memory_space=pltpu.VMEM)],
        scratch_shapes=[
            vmem((1024, 1024), f32), vmem((B, 512), f32), vmem((1024, 1024), bf16), vmem((1024, 1024), bf16), vmem((512, B), f32), vmem((64, 1024), f32),
            vmem((3, 64, 1024), f32), vmem((2, B, 1024), f32), vmem((2, B, 1024), bf16), vmem((2, B, 1024), bf16),
            vmem((2, B, 1024), f32), vmem((2, 3, 32, 1024), f32), vmem((2, B, 1024), f32),
            vmem((2, 8, B, B), f32), vmem((2, 3, 8, 32, B), f32),
            vmem((4, 8, 64, H), f32), vmem((2048, H), bf16), vmem((2048, H), bf16),
            vmem((B, 17 * B), f32), vmem((15, 8, 17 * B), f32), vmem((B, B), f32), vmem((8, 17 * B), f32),
            dma((7,)), dma((7,)), dma((2, 3)), dma((2, 3)), dma((2, 4)), dma((2, 3)), dma((2, 3)), dma((2, 3)), dma((2, 4)),
            dma((2, 4)), dma((2, 3)), dma((2, 3)), dma((2, 3)), dma((2, 3)), dma((2, 4)), dma((2, 4)), dma((3, 15)), dma((3, 15)),
            dma((3,)), dma((2,)), dma((3, 3)), dma((3, 3)), dma((3, 15)), dma((3, 15)), dma((3, 16)), dma((3, 16)),
        ],
        compiler_params=pltpu.CompilerParams(
            collective_id=0, has_side_effects=True, vmem_limit_bytes=63 * 1024 * 1024
        ),
    )(wavefunction, start_block)


def back_kernel(scale, q_ref, out_ref, mid, buf, s1, r1, s2, r2):
    row, col, layer = (lax.axis_index(n) for n in ("row", "col", "layer"))
    turns = [(lax.rem(row + n, 4), lax.rem(row + 4 - n, 4)) for n in range(1, 4)]
    sides = [(lax.rem(col + n, 4), lax.rem(col + 4 - n, 4)) for n in range(1, 4)]
    greet([(to, col, layer) for to, _ in turns] + [(row, to, layer) for to, _ in sides])
    sends = []
    for n, (to, _) in enumerate(turns):
        sends.append(send(q_ref.at[:, band(to, 512)], mid.at[n], s1.at[n], r1.at[n], (to, col, layer)))

    def pass_on(n, src, to):
        @pl.when(to == col)
        def _():
            buf[col] = src[...]

        @pl.when(to != col)
        def _():
            send(src, buf.at[col], s2.at[n], r2.at[lax.rem(to + 4 - col, 4) - 1], (row, to, layer))

    pass_on(0, q_ref.at[:, band(row, 512)], row)
    for n, (_, source) in enumerate(turns):
        done(mid.at[n], r1.at[n])
        pass_on(n + 1, mid.at[n], source)
    for n, (_, source) in enumerate(sides):
        done(buf.at[source], r2.at[n])
    for n in range(4):
        out_ref[n * 32 : (n + 1) * 32, :] = buf[n] * scale
    for s in sends:
        s.wait_send()
    for n, to in enumerate([row] + [source for _, source in turns]):

        @pl.when(to != col)
        def _():
            done(buf.at[0], s2.at[n])


def back(q, scale):
    dma = pltpu.SemaphoreType.DMA
    return pl.pallas_call(
        lambda *refs: back_kernel(scale, *refs),
        out_shape=jax.ShapeDtypeStruct((B, 512), f32),
        in_specs=[pl.BlockSpec(memory_space=pltpu.VMEM)],
        out_specs=pl.BlockSpec(memory_space=pltpu.VMEM),
        scratch_shapes=[
            pltpu.VMEM((3, 32, 512), f32), pltpu.VMEM((4, 32, 512), f32), dma((3,)), dma((3,)), dma((4,)), dma((3,)),
        ],
        compiler_params=pltpu.CompilerParams(collective_id=1, has_side_effects=True),
    )(q)


def factor(d_ref, y_ref, fill):
    lane = lax.broadcasted_iota(jnp.int32, (8, B), 1)
    sub = lax.broadcasted_iota(jnp.int32, (8, B), 0)
    full = lambda x: jnp.broadcast_to(x, (8, B))
    state = [d_ref[8 * i : 8 * i + 8, :] for i in range(16)]
    for b in range(8):
        base = 16 * b
        near = [[full(state[i][:, base + j : base + j + 1]) for i in range(2 * b, 2 * b + 2)] for j in range(16)]
        far = [[full(state[i][:, base + j : base + j + 1]) for i in range(2 * b + 2, 16)] for j in range(16)]
        turned = [near[j] + far[j] for j in range(16)]
        c = [[jnp.where(sub < 8, turned[j][h], 0.0) for h in range(2)] for j in range(16)]
        inside = (lane >= base) & (lane < base + 16)
        v = [jnp.where(inside, jnp.where(lane - base - 8 * h == sub, 1.0, 0.0), state[2 * b + h]) for h in range(2)]
        out, pivots, inverse = list(v), [c[0][0], c[8][1]], [1.0, 1.0]
        for j in range(16):
            h, s = divmod(j, 8)
            q = 1.0 / c[j][h]
            r = full(q[s : s + 1, :])
            out[h] = jnp.where(sub >= s, v[h], out[h])
            pivots[h] = jnp.where(sub >= s, c[j][h], pivots[h])
            inverse[h] = jnp.where(sub >= s, q, inverse[h])
            f = [c[j][g] * r for g in range(2)]
            f[h] = jnp.where(sub == s, 0.0, f[h])
            t = full(v[h][s : s + 1, :])
            v = [v[g] - f[g] * t for g in range(2)]
            for k in range(j + 1, 16):
                t = full(c[k][h][s : s + 1, :])
                c[k] = [c[k][g] - f[g] * t for g in range(2)]
        w = []
        for h in range(2):
            y_ref[base + 8 * h : base + 8 * h + 8, :] = jnp.where(lane <= base + 8 * h + sub, out[h] * lax.rsqrt(pivots[h]), 0.0)
            x = v[h] * inverse[h]
            w += [full(x[j : j + 1, :]) for j in range(8)]
        for i in range(2 * b + 2, 16):
            p = [turned[j][i - 2 * b] * w[j] for j in range(16)]
            while len(p) > 1:
                p = [p[k] + p[k + 1] for k in range(0, len(p), 2)]
            state[i] = jnp.where(inside, 0.0, state[i]) - p[0]
        fill(2 * b)
        fill(2 * b + 1)


def solve_kernel(g_ref, s_ref, q_ref, w, lhi, llo, yhi, ylo, d, y, sems):
    sizes = [((l + 1) * B, (16 - l) * B) for l in range(8)]

    def strip(s, first, n):
        l = min(s, 15 - s)

        @pl.loop(0, 16)
        def _(q):
            rows = pl.ds(pl.multiple_of(s * B + q * 8, 8), 8)
            pltpu.make_async_copy(g_ref.at[q, l, :, first : first + n], w.at[rows, 0:n], sems.at[s]).start()

    for l, (n, m) in enumerate(sizes):
        strip(l, 0, n)
    for l, (n, m) in reversed(list(enumerate(sizes))):
        strip(15 - l, n, m)

    slab = slice(16 * B, 16 * B + 32)
    w[slab, :] = s_ref[...]
    w[0:B, 7 * H : 8 * H] = jnp.zeros((B, H), f32)

    @pl.loop(0, 10)
    def _(i):
        lhi[band(i, H), :] = jnp.zeros((H, H), bf16)
        llo[band(i, H), :] = jnp.zeros((H, H), bf16)

    yhi[0:B, B:H] = jnp.zeros((B, B), bf16)
    ylo[0:B, B:H] = jnp.zeros((B, B), bf16)
    for l in range(2):
        done(w.at[l * B : (l + 1) * B, 0 : (l + 1) * B], sems.at[l])

    def nt3(a, b):
        (ahi, alo), (bhi, blo) = a, b
        return nt(ahi, bhi) + nt(ahi, blo) + nt(alo, bhi)

    def nn3(a, b):
        (ahi, alo), (bhi, blo) = a, b
        return nn(ahi, bhi) + nn(ahi, blo) + nn(alo, bhi)

    def keep(rows, x):
        lhi[rows, :], llo[rows, :] = split(x)

    def held(rows):
        return lhi[rows, :], llo[rows, :]

    def panel(rows, cols):
        p = nt3(split(w[rows, cols]), (yhi[...], ylo[...]))
        keep(rows, p)
        return p

    def tile(I, J, source, size=H):
        rows, cols = band(I, size), band(J, H)
        w[rows, cols] -= nt3(held(band(source, size)), held(cols))

    @pl.loop(0, 8)
    def _(K):
        c0 = pl.ds(pl.multiple_of(K * H, H), B)
        c1 = pl.ds(pl.multiple_of(K * H + B, B), B)
        both = band(K, H)
        side = 8 - K
        total = side * (side + 1) - 2

        def half(t):
            tri, pair = lax.div(t, 2), lax.rem(t, 2)
            n = jnp.int32(0)
            for step in range(1, 8):
                n = n + jnp.where(tri >= step * (step + 1) // 2, 1, 0)
            J = 7 - n
            I = 7 - (tri - lax.div(n * (n + 1), 2))
            real = (t < total) & (K > 0)
            tile(jnp.where(real, 2 * I + pair, 0), jnp.where(real, J, 7), jnp.where(real, 2 * I + pair, 18), B)

        def rows_of(b):
            J = K + b
            real = (J < 8) & (K > 0)
            cols = band(jnp.where(real, J, 7), H)
            source = pl.ds(pl.multiple_of(jnp.where(real, 16 * B, 18 * B), B), 32)
            w[slab, cols] -= nt3(held(source), held(cols))

        def fill(b):
            half(b)
            if b < 8:
                rows_of(b)

        d[...] = w[c0, c0]
        factor(d, y, fill)
        first = split(y[...])
        yhi[0:B, 0:B], ylo[0:B, 0:B] = first
        l21 = split(nt3(split(w[c1, c0]), first))
        d[...] = w[c1, c1] - nt3(l21, l21)
        corner = split(nn3(l21, first))
        factor(d, y, lambda b: half(16 + b))
        second = split(y[...])
        yhi[B:H, B:H], ylo[B:H, B:H] = second
        yhi[B:H, 0:B], ylo[B:H, 0:B] = split(-nn3(second, corner))

        @pl.when(K == 0)
        def _():
            for l in range(2, 16):
                done(w.at[l * B : (l + 1) * B, 0 : (l + 1) * B], sems.at[l])

        @pl.when(K > 0)
        def _():
            @pl.loop(16, jnp.maximum(lax.div(total, 2), 16))
            def _(t):
                half(2 * t)
                half(2 * t + 1)

        q_ref[:, both] = panel(slab, both)

        @pl.loop(K + 1, 8)
        def _(I):
            panel(band(I, H), both)

        @pl.when(K < 7)
        def _():
            rows = band(K + 1, H)
            w[rows, rows] -= nt3(held(rows), held(rows))


def solve(gram, slab):
    return pl.pallas_call(
        solve_kernel,
        out_shape=jax.ShapeDtypeStruct((32, 2048), f32),
        in_specs=[pl.BlockSpec(memory_space=pl.ANY), pl.BlockSpec(memory_space=pltpu.VMEM)],
        out_specs=pl.BlockSpec(memory_space=pltpu.VMEM),
        scratch_shapes=[
            pltpu.VMEM((16 * B + 32, 2048), f32), pltpu.VMEM((2560, H), bf16), pltpu.VMEM((2560, H), bf16),
            pltpu.VMEM((H, H), bf16), pltpu.VMEM((H, H), bf16),
            pltpu.VMEM((B, B), f32), pltpu.VMEM((B, B), f32), pltpu.SemaphoreType.DMA((16,)),
        ],
        compiler_params=pltpu.CompilerParams(vmem_limit_bytes=60 * 1024 * 1024),
    )(gram, slab)


def shards(wavefunction, start_block):
    gram, slab = front(wavefunction, start_block)
    gram = gram.reshape(16, 8, 8, 17 * B)
    return back(solve(gram, slab), math.sqrt(4096.0))


def solution(mesh):
    placed = (P("row", "col"), P(("col", "layer"), "row"))
    return jax.shard_map(
        shards, mesh=mesh, in_specs=placed, out_specs=P(("col", "layer"), "row"), check_vma=False
    )
```

```python
import math

import jax
import jax.numpy as jnp
from jax import lax
from jax.experimental import pallas as pl
from jax.experimental.pallas import tpu as pltpu
from jax.sharding import PartitionSpec as P

f32, bf16 = jnp.float32, jnp.bfloat16
B = 128
H = 256
MESH = pl.DeviceIdType.MESH


def split(x):
    hi = x.astype(bf16)
    return hi, (x - hi.astype(f32)).astype(bf16)


def nt(a, b):
    return lax.dot_general(a, b, (((1,), (1,)), ((), ())), preferred_element_type=f32)


def nn(a, b):
    return lax.dot_general(a, b, (((1,), (0,)), ((), ())), preferred_element_type=f32)


def band(i, size):
    return pl.ds(pl.multiple_of(i * size, size), size)


def done(ref, sem):
    pltpu.make_async_copy(ref, ref, sem).wait()


def greet(devices):
    barrier = pltpu.get_barrier_semaphore()
    for d in devices:
        pl.semaphore_signal(barrier, inc=1, device_id=d, device_id_type=MESH)
    pl.semaphore_wait(barrier, len(devices))


def send(src, dst, send_sem, recv_sem, device):
    copy = pltpu.make_async_remote_copy(
        src_ref=src, dst_ref=dst, send_sem=send_sem, recv_sem=recv_sem, device_id=device, device_id_type=MESH
    )
    copy.start()
    return copy


def front_kernel(
    psi_ref, start_ref, all_ref, slab_ref,
    psi, start,
    phi, plo, tile, bands, planes, st, shi, slo, tpart, tin, tfull, impart, imin, im, ihi, ilo, gpart, gin, turned, g_ref,
    s1, r1, s2, r2, s3, r3, sb, rb, sc, rc, sd, rd, se, re, sp, rp, sf, rf, own_sem, load_sem, sh, rh, si, ri, sj, rj,
):
    row, col, layer = (lax.axis_index(n) for n in ("row", "col", "layer"))
    group = 4 * row + col
    plane = [lax.rem(group + n, 16) for n in range(1, 16)]
    plane = [(lax.div(p, 4), lax.rem(p, 4), layer) for p in plane]
    loads = [pltpu.make_async_copy(start_ref, start, load_sem.at[0]), pltpu.make_async_copy(psi_ref, psi, load_sem.at[1])]
    for c in loads:
        c.start()
    greet(plane + [(row, col, lax.rem(layer + n, 8)) for n in range(1, 8)])
    loads[0].wait()
    for n in range(4):
        tile[n * B : (n + 1) * B, :] = start[:, n * B : (n + 1) * B].T
    for n in range(1, 8):
        to = lax.rem(layer + n, 8)
        (send(tile.at[band(to, 64), :], bands.at[:, band(layer, B)], s1, r1, (row, col, to)))
    bands[:, band(layer, B)] = tile[band(layer, 64), :]

    loads[1].wait()

    @pl.loop(0, 8)
    def _(i):
        rows = band(i, B)
        hi, lo = split(psi[rows, :])
        phi[rows, :] = hi
        plo[rows, :] = lo

    done(bands.at[:, 0 : 7 * B], r1)
    halves = [slice(h * 32, (h + 1) * 32) for h in range(2)]
    ups = [lax.rem(row + n, 4) for n in range(4)]
    downs = [lax.rem(row + 4 - n, 4) for n in range(4)]
    for h, part in enumerate(halves):
        for n in range(1, 4):
            to = lax.rem(col + n, 4)
            (send(bands.at[part, :], planes.at[n - 1, part, :], s2.at[h], r2.at[h, n - 1], (row, to, layer)))

    def pass_on(h, n, src):
        to = lax.rem(col + 4 - n, 4)
        dst = st.at[h, band(row, 32), :]

        @pl.when(to == row)
        def _():
            st[h, band(row, 32), :] = src[...]

        @pl.when(to != row)
        def _():
            send(src, dst, s3.at[h], r3.at[h], (to, col, layer))

    for h, part in enumerate(halves):
        pass_on(h, 0, bands.at[part, :])
        for n in range(1, 4):
            done(planes.at[n - 1, part, :], r2.at[h, n - 1])
            pass_on(h, n, planes.at[n - 1, part, :])
    for h in range(2):
        done(st.at[h, 0:96, :], r3.at[h])
        hi, lo = split(st[h])
        shi[h] = hi
        slo[h] = lo

        @pl.loop(0, 4)
        def _(i):
            cols = band(i, H)
            tpart[h, :, cols] = nn(shi[h], phi[:, cols]) + nn(shi[h], plo[:, cols]) + nn(slo[h], phi[:, cols])

        for n in range(1, 4):
            (send(
                tpart.at[h, band(ups[n], 32), :], tin.at[h, n - 1], sb.at[h], rb.at[h], (ups[n], col, layer)
            ))
    for h in range(2):
        done(tin.at[h], rb.at[h])
        mine = band(row, 32)
        tfull[h, mine, :] = (tpart[h, mine, :] + tin[h, 0]) + (tin[h, 1] + tin[h, 2])
        for n in (1, 3):
            mine = tfull.at[h, band(row, 32), :]
            (send(mine, mine, sc.at[h], rc.at[h, n - 1], (ups[n], col, layer)))
    for h in range(2):
        for n, skip in ((1, 0), (3, 16)):
            done(tfull.at[h, band(downs[n], 32), :], rc.at[h, n - 1])
            near = tfull.at[h, pl.ds(pl.multiple_of(downs[n] * 32 + skip, 16), 16), :]
            slot = 1 if n == 1 else 3
            (send(near, near, sc.at[h], rc.at[h, slot], (ups[n], col, layer)))
    for h in range(2):
        for slot, skip in ((1, 0), (3, 16)):
            done(tfull.at[h, pl.ds(pl.multiple_of(ups[2] * 32 + skip, 16), 16), :], rc.at[h, slot])
        hi, lo = split(tfull[h])
        shi[h] = hi
        slo[h] = lo

        @pl.loop(0, 4)
        def _(i):
            rows = band(i, H)
            p = nt(phi[rows, :], shi[h]) + nt(plo[rows, :], shi[h]) + nt(phi[rows, :], slo[h])
            impart[h, pl.ds(2 * i, 2)] = p.reshape(2, B, B)

        for n in range(1, 4):
            to = lax.rem(col + n, 4)
            (send(
                impart.at[h, :, band(to, 32), :], imin.at[h, n - 1], sd.at[h], rd.at[h], (row, to, layer)
            ))
    other = (row, col, layer + 1 - 2 * lax.rem(layer, 2))
    for h, part in enumerate(halves):
        done(imin.at[h], rd.at[h])
        own = (impart[h, :, band(col, 32), :] + imin[h, 0]) + (imin[h, 1] + imin[h, 2])
        im[:, layer, part] = own.reshape(H, B).T.reshape(4, 32, H)
        mine = im.at[:, layer, part]
        for n in range(1, 4):
            to = lax.rem(layer + 2 * n, 8)
            (send(mine, mine, se.at[h], re.at[h, n - 1], (row, col, to)))
        (send(mine, mine, sp.at[h], rp.at[h], other))
    for h, part in enumerate(halves):
        for n in (1, 3, 2):
            came = im.at[:, lax.rem(layer + 8 - 2 * n, 8), part]
            done(came, re.at[h, n - 1])
            (send(came, came, sp.at[h], rp.at[h], other))
    for h, part in enumerate(halves):
        done(im.at[:, 0:4, part], rp.at[h])
    for n in range(4):
        rows = slice(n * 512, (n + 1) * 512)
        hi, lo = split(im[n].reshape(512, H))
        ihi[rows, :] = hi
        ilo[rows, :] = lo

    @pl.loop(0, 17)
    def _(t):
        first = t <= layer
        i = band(jnp.where(first, layer, 15 - layer), B)
        j = band(jnp.where(first, t, t - layer - 1), B)
        gpart[:, band(t, B)] = nt(ihi[i, :], ihi[j, :]) + nt(ihi[i, :], ilo[j, :]) + nt(ilo[i, :], ihi[j, :])

    parts = [("xyz", slice(0, 6 * B)), ("yzx", slice(6 * B, 12 * B)), ("zxy", slice(12 * B, 17 * B))]
    for c, (order, lanes) in enumerate(parts):
        for n in range(1, 16):
            to = lax.rem(group + n, 16)
            (send(
                gpart.at[band(to, 8), lanes], gin.at[n - 1, :, lanes], sf, rf.at[c], plane[n - 1]
            ))
    lanes = band(lax.div(layer, 4), B)
    for n in range(16):
        turned[...] = im[n // 4, 2 * (n % 4) : 2 * (n % 4) + 2, :, lanes].reshape(B, B).T
        slab_ref[:, n * B : (n + 1) * B] = turned[band(lax.rem(layer, 4), 32), :]
    x, core = lax.div(layer, 2), lax.rem(layer, 2)
    at = {"z": row, "y": col, "x": x}
    spots = []

    def device(place):
        return (place["z"], place["y"], 2 * place["x"] + core)

    def away(axis, n):
        return {**at, axis: lax.rem(at[axis] + n + 4, 4)}

    def cells(place, lanes, k=core, along=None):
        index = [slice(None) if a == along else place[a] for a in "zyx"]
        return all_ref.at[index[0], index[1], index[2], k, :, lanes]

    for c, (order, lanes) in enumerate(parts):
        total = gpart[band(group, 8), lanes]
        done(gin.at[:, :, lanes], rf.at[c])
        for n in range(15):
            total = total + gin[n, :, lanes]
        g_ref[:, lanes] = total
        pltpu.make_async_copy(g_ref.at[:, lanes], cells(at, lanes), own_sem.at[c]).start()
        for n in range(1, 4):
            (send(g_ref.at[:, lanes], cells(at, lanes), sh.at[c], rh.at[c], device(away(order[0], n))))

    def line(c, place):
        order, lanes = parts[c]
        return cells(place, lanes, along=order[0])

    def share(c, place, slot):
        order, lanes = parts[c]
        src = cells(place, lanes, along=order[0])
        (send(src, src, sj.at[c], rj.at[c], (row, col, layer + 1 - 2 * core)))

    def outward(c, place, j, directions):
        src = line(c, place)
        for d in directions:
            slot = 3 + j + (0 if d == 1 else 6)
            (send(src, src, si.at[c, 1], ri.at[c, slot], device(away(parts[c][0][2], d))))

    for c, (order, lanes) in enumerate(parts):
        done(all_ref.at[0, 0, 0:3, 0, :, lanes], rh.at[c])
        done(g_ref.at[:, lanes], own_sem.at[c])
        for n in range(1, 4):
            (send(line(c, at), line(c, at), si.at[c, 0], ri.at[c, n - 1], device(away(order[1], n))))
        outward(c, at, 0, (1, -1))
        share(c, at, 0)
    for n in range(1, 4):
        for c, (order, lanes) in enumerate(parts):
            place = away(order[1], -n)
            done(line(c, place), ri.at[c, n - 1])
            outward(c, place, n, (1, -1))
            share(c, place, n)
    for n in range(4):
        for c, (order, lanes) in enumerate(parts):
            for d in (1, -1):
                place = {**away(order[1], -n), order[2]: lax.rem(at[order[2]] - d + 4, 4)}
                done(line(c, place), ri.at[c, 3 + n + (0 if d == 1 else 6)])
                if (n < 2) == (d == 1):
                    src = line(c, place)
                    slot = 3 + 4 + n % 2 + (0 if d == 1 else 6)
                    (send(src, src, si.at[c, 1], ri.at[c, slot], device(away(order[2], d))))
                share(c, place, 4 + n + (0 if d == 1 else 4))
    for n in range(4):
        for c, (order, lanes) in enumerate(parts):
            d = 1 if n < 2 else -1
            place = {**away(order[1], -n), order[2]: lax.rem(at[order[2]] + 2, 4)}
            done(line(c, place), ri.at[c, 3 + 4 + n % 2 + (0 if d == 1 else 6)])
            share(c, place, 12 + n)
    for c, (order, lanes) in enumerate(parts):
        done(all_ref.at[:, :, :, 0, :, lanes], rj.at[c])
    done(tile.at[0 : 7 * 64, :], s1)
    for h, part in enumerate(halves):
        done(planes.at[:, part, :], s2.at[h])
        done(st.at[h, 0:96, :], s3.at[h])
        done(tin.at[h], sb.at[h])
        done(tfull.at[h, 0:96, :], sc.at[h])
        done(imin.at[h], sd.at[h])
        done(im.at[:, 0:3, part], se.at[h])
        done(im.at[:, 0:4, part], sp.at[h])
    done(gin, sf)
    for c, (order, lanes) in enumerate(parts):
        done(all_ref.at[0, 0, 0:3, 0, :, lanes], sh.at[c])
        done(all_ref.at[0, 0:3, :, 0, :, lanes], si.at[c, 0])
        done(all_ref.at[0:3, :, :, 0, :, lanes], si.at[c, 1])
        done(all_ref.at[:, :, :, 0, :, lanes], sj.at[c])


def front(wavefunction, start_block):
    dma = pltpu.SemaphoreType.DMA
    vmem = pltpu.VMEM
    return pl.pallas_call(
        front_kernel,
        out_shape=(jax.ShapeDtypeStruct((4, 4, 4, 2, 8, 17 * B), f32), jax.ShapeDtypeStruct((32, 2048), f32)),
        in_specs=[pl.BlockSpec(memory_space=pl.ANY)] * 2,
        out_specs=[pl.BlockSpec(memory_space=pl.ANY), pl.BlockSpec(memory_space=pltpu.VMEM)],
        scratch_shapes=[
            vmem((1024, 1024), f32), vmem((B, 512), f32), vmem((1024, 1024), bf16), vmem((1024, 1024), bf16), vmem((512, B), f32), vmem((64, 1024), f32),
            vmem((3, 64, 1024), f32), vmem((2, B, 1024), f32), vmem((2, B, 1024), bf16), vmem((2, B, 1024), bf16),
            vmem((2, B, 1024), f32), vmem((2, 3, 32, 1024), f32), vmem((2, B, 1024), f32),
            vmem((2, 8, B, B), f32), vmem((2, 3, 8, 32, B), f32),
            vmem((4, 8, 64, H), f32), vmem((2048, H), bf16), vmem((2048, H), bf16),
            vmem((B, 17 * B), f32), vmem((15, 8, 17 * B), f32), vmem((B, B), f32), vmem((8, 17 * B), f32),
            dma, dma, dma((2,)), dma((2, 3)), dma((2,)), dma((2,)), dma((2,)), dma((2,)), dma((2,)), dma((2, 4)),
            dma((2,)), dma((2,)), dma((2,)), dma((2, 3)), dma((2,)), dma((2,)), dma, dma((3,)),
            dma((3,)), dma((2,)), dma((3,)), dma((3,)), dma((3, 2)), dma((3, 15)), dma((3,)), dma((3,)),
        ],
        compiler_params=pltpu.CompilerParams(
            collective_id=0, has_side_effects=True, vmem_limit_bytes=63 * 1024 * 1024
        ),
    )(wavefunction, start_block)


def back_kernel(scale, q_ref, out_ref, mid, buf, s1, r1, s2, r2):
    row, col, layer = (lax.axis_index(n) for n in ("row", "col", "layer"))
    turns = [(lax.rem(row + n, 4), lax.rem(row + 4 - n, 4)) for n in range(1, 4)]
    sides = [(lax.rem(col + n, 4), lax.rem(col + 4 - n, 4)) for n in range(1, 4)]
    greet([(to, col, layer) for to, _ in turns] + [(row, to, layer) for to, _ in sides])
    sends = []
    for n, (to, _) in enumerate(turns):
        sends.append(send(q_ref.at[:, band(to, 512)], mid.at[n], s1.at[n], r1.at[n], (to, col, layer)))

    def pass_on(n, src, to):
        @pl.when(to == col)
        def _():
            buf[col] = src[...]

        @pl.when(to != col)
        def _():
            send(src, buf.at[col], s2.at[n], r2.at[lax.rem(to + 4 - col, 4) - 1], (row, to, layer))

    pass_on(0, q_ref.at[:, band(row, 512)], row)
    for n, (_, source) in enumerate(turns):
        done(mid.at[n], r1.at[n])
        pass_on(n + 1, mid.at[n], source)
    for n, (_, source) in enumerate(sides):
        done(buf.at[source], r2.at[n])
    for n in range(4):
        out_ref[n * 32 : (n + 1) * 32, :] = buf[n] * scale
    for s in sends:
        s.wait_send()
    for n, to in enumerate([row] + [source for _, source in turns]):

        @pl.when(to != col)
        def _():
            done(buf.at[0], s2.at[n])


def back(q, scale):
    dma = pltpu.SemaphoreType.DMA
    return pl.pallas_call(
        lambda *refs: back_kernel(scale, *refs),
        out_shape=jax.ShapeDtypeStruct((B, 512), f32),
        in_specs=[pl.BlockSpec(memory_space=pltpu.VMEM)],
        out_specs=pl.BlockSpec(memory_space=pltpu.VMEM),
        scratch_shapes=[
            pltpu.VMEM((3, 32, 512), f32), pltpu.VMEM((4, 32, 512), f32), dma((3,)), dma((3,)), dma((4,)), dma((3,)),
        ],
        compiler_params=pltpu.CompilerParams(collective_id=1, has_side_effects=True),
    )(q)


def factor(d_ref, y_ref, fill):
    lane = lax.broadcasted_iota(jnp.int32, (8, B), 1)
    sub = lax.broadcasted_iota(jnp.int32, (8, B), 0)
    full = lambda x: jnp.broadcast_to(x, (8, B))
    state = [d_ref[8 * i : 8 * i + 8, :] for i in range(16)]
    for b in range(8):
        base = 16 * b
        near = [[full(state[i][:, base + j : base + j + 1]) for i in range(2 * b, 2 * b + 2)] for j in range(16)]
        far = [[full(state[i][:, base + j : base + j + 1]) for i in range(2 * b + 2, 16)] for j in range(16)]
        turned = [near[j] + far[j] for j in range(16)]
        c = [[jnp.where(sub < 8, turned[j][h], 0.0) for h in range(2)] for j in range(16)]
        inside = (lane >= base) & (lane < base + 16)
        v = [jnp.where(inside, jnp.where(lane - base - 8 * h == sub, 1.0, 0.0), state[2 * b + h]) for h in range(2)]
        out, pivots, inverse = list(v), [c[0][0], c[8][1]], [1.0, 1.0]
        for j in range(16):
            h, s = divmod(j, 8)
            q = 1.0 / c[j][h]
            r = full(q[s : s + 1, :])
            out[h] = jnp.where(sub >= s, v[h], out[h])
            pivots[h] = jnp.where(sub >= s, c[j][h], pivots[h])
            inverse[h] = jnp.where(sub >= s, q, inverse[h])
            f = [c[j][g] * r for g in range(2)]
            f[h] = jnp.where(sub == s, 0.0, f[h])
            t = full(v[h][s : s + 1, :])
            v = [v[g] - f[g] * t for g in range(2)]
            for k in range(j + 1, 16):
                t = full(c[k][h][s : s + 1, :])
                c[k] = [c[k][g] - f[g] * t for g in range(2)]
        w = []
        for h in range(2):
            y_ref[base + 8 * h : base + 8 * h + 8, :] = jnp.where(lane <= base + 8 * h + sub, out[h] * lax.rsqrt(pivots[h]), 0.0)
            x = v[h] * inverse[h]
            w += [full(x[j : j + 1, :]) for j in range(8)]
        for i in range(2 * b + 2, 16):
            p = [turned[j][i - 2 * b] * w[j] for j in range(16)]
            while len(p) > 1:
                p = [p[k] + p[k + 1] for k in range(0, len(p), 2)]
            state[i] = jnp.where(inside, 0.0, state[i]) - p[0]
        fill(2 * b)
        fill(2 * b + 1)


def solve_kernel(plan, g_ref, s_ref, q_ref, w, lhi, llo, yhi, ylo, d, y, sems):
    sizes = [((l + 1) * B, (16 - l) * B) for l in range(8)]

    def strip(s, first, n):
        l = min(s, 15 - s)

        @pl.loop(0, 16)
        def _(q):
            rows = pl.ds(pl.multiple_of(s * B + q * 8, 8), 8)
            pltpu.make_async_copy(g_ref.at[q, l, :, first : first + n], w.at[rows, 0:n], sems.at[s]).start()

    for l, (n, m) in enumerate(sizes):
        strip(l, 0, n)
    for l, (n, m) in reversed(list(enumerate(sizes))):
        strip(15 - l, n, m)

    slab = slice(16 * B, 16 * B + 32)
    w[slab, :] = s_ref[...]
    w[0:B, 7 * H : 8 * H] = jnp.zeros((B, H), f32)

    @pl.loop(0, 10)
    def _(i):
        for part in (lhi, llo):
            part[band(i, H), 0:H] = jnp.zeros((H, H), bf16)

    @pl.loop(1, 8)
    def _(i):
        for part in (lhi, llo):
            part[18 * B : 20 * B, band(i, H)] = jnp.zeros((H, H), bf16)
            part[14 * B : 16 * B, band(i, H)] = jnp.zeros((H, H), bf16)

    yhi[0:B, B:H] = jnp.zeros((B, B), bf16)
    ylo[0:B, B:H] = jnp.zeros((B, B), bf16)
    for l in range(2):
        done(w.at[l * B : (l + 1) * B, 0 : (l + 1) * B], sems.at[l])

    def nt3(a, b):
        (ahi, alo), (bhi, blo) = a, b
        return nt(ahi, bhi) + nt(ahi, blo) + nt(alo, bhi)

    def nn3(a, b):
        (ahi, alo), (bhi, blo) = a, b
        return nn(ahi, bhi) + nn(ahi, blo) + nn(alo, bhi)

    def held(rows, cols):
        return lhi[rows, cols], llo[rows, cols]

    def panel(rows, cols):
        p = nt3(split(w[rows, cols]), (yhi[...], ylo[...]))
        lhi[rows, cols], llo[rows, cols] = split(p)
        return p

    @pl.loop(0, 8)
    def _(K):
        c0 = pl.ds(pl.multiple_of(K * H, H), B)
        c1 = pl.ds(pl.multiple_of(K * H + B, B), B)
        both = band(K, H)
        def half(t):
            code = plan[K * 32 + t]
            i, J, source = lax.div(code, 256), lax.rem(lax.div(code, 16), 16), lax.rem(code, 16)
            rows, cols, old = band(lax.rem(i, 18), B), band(J, H), band(source, H)
            w[rows, cols] -= nt3(held(band(i, B), old), held(cols, old))

        def rows_of(b):
            J = K + b
            real = (J < 8) & (K > 0)
            cols = band(jnp.where(real, J, 7), H)
            source = pl.ds(pl.multiple_of(jnp.where(real, 16 * B, 18 * B), B), 32)
            old = band(jnp.maximum(K - 1, 0), H)
            w[slab, cols] -= nt3(held(source, old), held(cols, old))

        def fill(b):
            half(b)
            if b < 8:
                rows_of(b)

        d[...] = w[c0, c0]
        factor(d, y, fill)
        first = split(y[...])
        yhi[0:B, 0:B], ylo[0:B, 0:B] = first
        l21 = split(nt3(split(w[c1, c0]), first))
        d[...] = w[c1, c1] - nt3(l21, l21)
        corner = split(nn3(l21, first))
        factor(d, y, lambda b: half(16 + b))
        second = split(y[...])
        yhi[B:H, B:H], ylo[B:H, B:H] = second
        yhi[B:H, 0:B], ylo[B:H, 0:B] = split(-nn3(second, corner))

        @pl.when(K == 0)
        def _():
            for l in range(2, 16):
                done(w.at[l * B : (l + 1) * B, 0 : (l + 1) * B], sems.at[l])

        q_ref[:, both] = panel(slab, both)

        @pl.loop(K + 1, 8)
        def _(I):
            panel(band(I, H), both)

        @pl.when(K < 7)
        def _():
            rows = band(K + 1, H)
            w[rows, rows] -= nt3(held(rows, both), held(rows, both))


def schedule():
    plan, waiting = [], []
    blank = 18 * 256 + 7 * 16
    for K in range(8):
        if K:
            waiting += [
                (J, K - 1, i) for J in range(K, 8) for i in range(2 * J, 16) if not (J == K and i < 2 * J + 2)
            ]
        waiting.sort()
        now, waiting = waiting[:32], waiting[32:]
        assert all(J > K + 1 or (J > K and i >= 2 * J + 2) for J, _, i in waiting)
        plan += [i * 256 + J * 16 + source for J, source, i in now] + [blank] * (32 - len(now))
    return jnp.array(plan, jnp.int32)


def solve(gram, slab):
    return pl.pallas_call(
        solve_kernel,
        out_shape=jax.ShapeDtypeStruct((32, 2048), f32),
        in_specs=[
            pl.BlockSpec(memory_space=pltpu.SMEM), pl.BlockSpec(memory_space=pl.ANY), pl.BlockSpec(memory_space=pltpu.VMEM),
        ],
        out_specs=pl.BlockSpec(memory_space=pltpu.VMEM),
        scratch_shapes=[
            pltpu.VMEM((16 * B + 32, 2048), f32), pltpu.VMEM((2560, 2048), bf16), pltpu.VMEM((2560, 2048), bf16),
            pltpu.VMEM((H, H), bf16), pltpu.VMEM((H, H), bf16),
            pltpu.VMEM((B, B), f32), pltpu.VMEM((B, B), f32), pltpu.SemaphoreType.DMA((16,)),
        ],
        compiler_params=pltpu.CompilerParams(vmem_limit_bytes=60 * 1024 * 1024),
    )(schedule(), gram, slab)


def shards(wavefunction, start_block):
    gram, slab = front(wavefunction, start_block)
    gram = gram.reshape(16, 8, 8, 17 * B)
    return back(solve(gram, slab), math.sqrt(4096.0))


def solution(mesh):
    placed = (P("row", "col"), P(("col", "layer"), "row"))
    return jax.shard_map(
        shards, mesh=mesh, in_specs=placed, out_specs=P(("col", "layer"), "row"), check_vma=False
    )
```

```python
import math

import jax
import jax.numpy as jnp
from jax import lax
from jax.experimental import pallas as pl
from jax.experimental.pallas import tpu as pltpu
from jax.sharding import PartitionSpec as P

f32, bf16 = jnp.float32, jnp.bfloat16
B = 128
H = 256
MESH = pl.DeviceIdType.MESH


def split(x):
    hi = x.astype(bf16)
    return hi, (x - hi.astype(f32)).astype(bf16)


def nt(a, b):
    return lax.dot_general(a, b, (((1,), (1,)), ((), ())), preferred_element_type=f32)


def nn(a, b):
    return lax.dot_general(a, b, (((1,), (0,)), ((), ())), preferred_element_type=f32)


def band(i, size):
    return pl.ds(pl.multiple_of(i * size, size), size)


def done(ref, sem):
    pltpu.make_async_copy(ref, ref, sem).wait()


def greet(devices):
    barrier = pltpu.get_barrier_semaphore()
    for d in devices:
        pl.semaphore_signal(barrier, inc=1, device_id=d, device_id_type=MESH)
    pl.semaphore_wait(barrier, len(devices))


def send(src, dst, send_sem, recv_sem, device):
    copy = pltpu.make_async_remote_copy(
        src_ref=src, dst_ref=dst, send_sem=send_sem, recv_sem=recv_sem, device_id=device, device_id_type=MESH
    )
    copy.start()
    return copy


def front_kernel(
    psi_ref, start_ref, all_ref, slab_ref,
    psi, start,
    phi, plo, tile, bands, mid, st, shi, slo, tpart, tin, tfull, impart, imin, im, ihi, ilo, gpart, gin, turned, g_ref,
    s1, r1, s2, r2, s3, r3, s4, r4, sb, rb, sc, rc, sd, rd, se, re, sp, rp, sf, rf, own_sem, load_sem, sh, rh, si, ri, sj, rj,
):
    row, col, layer = (lax.axis_index(n) for n in ("row", "col", "layer"))
    group = 4 * row + col
    plane = [lax.rem(group + n, 16) for n in range(1, 16)]
    plane = [(lax.div(p, 4), lax.rem(p, 4), layer) for p in plane]
    loads = [pltpu.make_async_copy(start_ref, start, load_sem.at[0]), pltpu.make_async_copy(psi_ref, psi, load_sem.at[1])]
    for c in loads:
        c.start()
    greet(plane + [(row, col, lax.rem(layer + n, 8)) for n in range(1, 8)])
    loads[0].wait()
    for n in range(4):
        tile[n * B : (n + 1) * B, :] = start[:, n * B : (n + 1) * B].T
    for n in range(1, 8):
        to = lax.rem(layer + n, 8)
        (send(tile.at[band(to, 64), :], bands.at[:, band(layer, B)], s1, r1, (row, col, to)))
    bands[:, band(layer, B)] = tile[band(layer, 64), :]

    loads[1].wait()

    @pl.loop(0, 8)
    def _(i):
        rows = band(i, B)
        hi, lo = split(psi[rows, :])
        phi[rows, :] = hi
        plo[rows, :] = lo

    done(bands.at[:, 0 : 7 * B], r1)
    halves = [slice(h * 32, (h + 1) * 32) for h in range(2)]
    ups = [lax.rem(row + n, 4) for n in range(4)]
    downs = [lax.rem(row + 4 - n, 4) for n in range(4)]
    for h in range(2):
        for n in range(1, 4):
            to = lax.rem(col + n, 4)
            send(bands.at[band(4 * h + to, 8), :], mid.at[h, col], s2.at[h], r2.at[h], (row, to, layer))
        mid[h, col] = bands[band(4 * h + col, 8), :]
    for h in range(2):
        done(mid.at[h, 0:3], r2.at[h])
        for n in range(1, 4):
            send(mid.at[h, ups[n]], st.at[h, row, col], s3.at[h], r3.at[h], (ups[n], col, layer))
        st[h, row, col] = mid[h, row]
    for h in range(2):
        done(mid.at[h, 0:3], r3.at[h])
        for n in range(1, 4):
            mine = st.at[h, :, col]
            send(mine, mine, s4.at[h], r4.at[h], (row, lax.rem(col + n, 4), layer))
    for h in range(2):
        done(st.at[h, :, 0:3], r4.at[h])
        hi, lo = split(st[h].reshape(B, 1024))
        shi[h] = hi
        slo[h] = lo

        @pl.loop(0, 4)
        def _(i):
            cols = band(i, H)
            tpart[h, :, cols] = nn(shi[h], phi[:, cols]) + nn(shi[h], plo[:, cols]) + nn(slo[h], phi[:, cols])

        for n in range(1, 4):
            (send(
                tpart.at[h, band(ups[n], 32), :], tin.at[h, n - 1], sb.at[h], rb.at[h], (ups[n], col, layer)
            ))
    for h in range(2):
        done(tin.at[h], rb.at[h])
        mine = band(row, 32)
        tfull[h, mine, :] = (tpart[h, mine, :] + tin[h, 0]) + (tin[h, 1] + tin[h, 2])
        for n in (1, 3):
            mine = tfull.at[h, band(row, 32), :]
            (send(mine, mine, sc.at[h], rc.at[h, n - 1], (ups[n], col, layer)))
    for h in range(2):
        for n, skip in ((1, 0), (3, 16)):
            done(tfull.at[h, band(downs[n], 32), :], rc.at[h, n - 1])
            near = tfull.at[h, pl.ds(pl.multiple_of(downs[n] * 32 + skip, 16), 16), :]
            slot = 1 if n == 1 else 3
            (send(near, near, sc.at[h], rc.at[h, slot], (ups[n], col, layer)))
    for h in range(2):
        for slot, skip in ((1, 0), (3, 16)):
            done(tfull.at[h, pl.ds(pl.multiple_of(ups[2] * 32 + skip, 16), 16), :], rc.at[h, slot])
        hi, lo = split(tfull[h])
        shi[h] = hi
        slo[h] = lo

        @pl.loop(0, 4)
        def _(i):
            rows = band(i, H)
            p = nt(phi[rows, :], shi[h]) + nt(plo[rows, :], shi[h]) + nt(phi[rows, :], slo[h])
            impart[h, pl.ds(2 * i, 2)] = p.reshape(2, B, B)

        for n in range(1, 4):
            to = lax.rem(col + n, 4)
            (send(
                impart.at[h, :, band(to, 32), :], imin.at[h, n - 1], sd.at[h], rd.at[h], (row, to, layer)
            ))
    other = (row, col, layer + 1 - 2 * lax.rem(layer, 2))
    for h, part in enumerate(halves):
        done(imin.at[h], rd.at[h])
        own = (impart[h, :, band(col, 32), :] + imin[h, 0]) + (imin[h, 1] + imin[h, 2])
        im[:, layer, part] = own.reshape(H, B).T.reshape(4, 32, H)
        mine = im.at[:, layer, part]
        for n in range(1, 4):
            to = lax.rem(layer + 2 * n, 8)
            (send(mine, mine, se.at[h], re.at[h, n - 1], (row, col, to)))
        (send(mine, mine, sp.at[h], rp.at[h], other))
    for h, part in enumerate(halves):
        for n in (1, 3, 2):
            came = im.at[:, lax.rem(layer + 8 - 2 * n, 8), part]
            done(came, re.at[h, n - 1])
            (send(came, came, sp.at[h], rp.at[h], other))
    for h, part in enumerate(halves):
        done(im.at[:, 0:4, part], rp.at[h])
    for n in range(4):
        rows = slice(n * 512, (n + 1) * 512)
        hi, lo = split(im[n].reshape(512, H))
        ihi[rows, :] = hi
        ilo[rows, :] = lo

    parts = [("xyz", slice(0, 6 * B)), ("yzx", slice(6 * B, 12 * B)), ("zxy", slice(12 * B, 17 * B))]
    for c, (order, lanes) in enumerate(parts):

        @pl.loop(lanes.start // B, lanes.stop // B)
        def _(t):
            first = t <= layer
            i = band(jnp.where(first, layer, 15 - layer), B)
            j = band(jnp.where(first, t, t - layer - 1), B)
            gpart[:, band(t, B)] = nt(ihi[i, :], ihi[j, :]) + nt(ihi[i, :], ilo[j, :]) + nt(ilo[i, :], ihi[j, :])

        for n in range(1, 16):
            to = lax.rem(group + n, 16)
            send(gpart.at[band(to, 8), lanes], gin.at[n - 1, :, lanes], sf, rf.at[c], plane[n - 1])
    lanes = band(lax.div(layer, 4), B)
    for n in range(16):
        turned[...] = im[n // 4, 2 * (n % 4) : 2 * (n % 4) + 2, :, lanes].reshape(B, B).T
        slab_ref[:, n * B : (n + 1) * B] = turned[band(lax.rem(layer, 4), 32), :]
    x, core = lax.div(layer, 2), lax.rem(layer, 2)
    at = {"z": row, "y": col, "x": x}
    spots = []

    def device(place):
        return (place["z"], place["y"], 2 * place["x"] + core)

    def away(axis, n):
        return {**at, axis: lax.rem(at[axis] + n + 4, 4)}

    def cells(place, lanes, k=core, along=None):
        index = [slice(None) if a == along else place[a] for a in "zyx"]
        return all_ref.at[index[0], index[1], index[2], k, :, lanes]

    for c, (order, lanes) in enumerate(parts):
        total = gpart[band(group, 8), lanes]
        done(gin.at[:, :, lanes], rf.at[c])
        for n in range(15):
            total = total + gin[n, :, lanes]
        g_ref[:, lanes] = total
        pltpu.make_async_copy(g_ref.at[:, lanes], cells(at, lanes), own_sem.at[c]).start()
        for n in range(1, 4):
            (send(g_ref.at[:, lanes], cells(at, lanes), sh.at[c], rh.at[c], device(away(order[0], n))))

    def line(c, place):
        order, lanes = parts[c]
        return cells(place, lanes, along=order[0])

    def share(c, place, slot):
        order, lanes = parts[c]
        src = cells(place, lanes, along=order[0])
        (send(src, src, sj.at[c], rj.at[c], (row, col, layer + 1 - 2 * core)))

    def outward(c, place, j, directions):
        src = line(c, place)
        for d in directions:
            slot = 3 + j + (0 if d == 1 else 6)
            (send(src, src, si.at[c, 1], ri.at[c, slot], device(away(parts[c][0][2], d))))

    for c, (order, lanes) in enumerate(parts):
        done(all_ref.at[0, 0, 0:3, 0, :, lanes], rh.at[c])
        done(g_ref.at[:, lanes], own_sem.at[c])
        for n in range(1, 4):
            (send(line(c, at), line(c, at), si.at[c, 0], ri.at[c, n - 1], device(away(order[1], n))))
        outward(c, at, 0, (1, -1))
        share(c, at, 0)
    for n in range(1, 4):
        for c, (order, lanes) in enumerate(parts):
            place = away(order[1], -n)
            done(line(c, place), ri.at[c, n - 1])
            outward(c, place, n, (1, -1))
            share(c, place, n)
    for n in range(4):
        for c, (order, lanes) in enumerate(parts):
            for d in (1, -1):
                place = {**away(order[1], -n), order[2]: lax.rem(at[order[2]] - d + 4, 4)}
                done(line(c, place), ri.at[c, 3 + n + (0 if d == 1 else 6)])
                if (n < 2) == (d == 1):
                    src = line(c, place)
                    slot = 3 + 4 + n % 2 + (0 if d == 1 else 6)
                    (send(src, src, si.at[c, 1], ri.at[c, slot], device(away(order[2], d))))
                share(c, place, 4 + n + (0 if d == 1 else 4))
    for n in range(4):
        for c, (order, lanes) in enumerate(parts):
            d = 1 if n < 2 else -1
            place = {**away(order[1], -n), order[2]: lax.rem(at[order[2]] + 2, 4)}
            done(line(c, place), ri.at[c, 3 + 4 + n % 2 + (0 if d == 1 else 6)])
            share(c, place, 12 + n)
    for c, (order, lanes) in enumerate(parts):
        done(all_ref.at[:, :, :, 0, :, lanes], rj.at[c])
    done(tile.at[0 : 7 * 64, :], s1)
    for h, part in enumerate(halves):
        done(mid.at[h, 0:3], s2.at[h])
        done(mid.at[h, 0:3], s3.at[h])
        done(st.at[h, :, 0:3], s4.at[h])
        done(tin.at[h], sb.at[h])
        done(tfull.at[h, 0:96, :], sc.at[h])
        done(imin.at[h], sd.at[h])
        done(im.at[:, 0:3, part], se.at[h])
        done(im.at[:, 0:4, part], sp.at[h])
    done(gin, sf)
    for c, (order, lanes) in enumerate(parts):
        done(all_ref.at[0, 0, 0:3, 0, :, lanes], sh.at[c])
        done(all_ref.at[0, 0:3, :, 0, :, lanes], si.at[c, 0])
        done(all_ref.at[0:3, :, :, 0, :, lanes], si.at[c, 1])
        done(all_ref.at[:, :, :, 0, :, lanes], sj.at[c])


def front(wavefunction, start_block):
    dma = pltpu.SemaphoreType.DMA
    vmem = pltpu.VMEM
    return pl.pallas_call(
        front_kernel,
        out_shape=(jax.ShapeDtypeStruct((4, 4, 4, 2, 8, 17 * B), f32), jax.ShapeDtypeStruct((32, 2048), f32)),
        in_specs=[pl.BlockSpec(memory_space=pl.ANY)] * 2,
        out_specs=[pl.BlockSpec(memory_space=pl.ANY), pl.BlockSpec(memory_space=pltpu.VMEM)],
        scratch_shapes=[
            vmem((1024, 1024), f32), vmem((B, 512), f32), vmem((1024, 1024), bf16), vmem((1024, 1024), bf16), vmem((512, B), f32), vmem((64, 1024), f32),
            vmem((2, 4, 8, 1024), f32), vmem((2, 4, 4, 8, 1024), f32), vmem((2, B, 1024), bf16), vmem((2, B, 1024), bf16),
            vmem((2, B, 1024), f32), vmem((2, 3, 32, 1024), f32), vmem((2, B, 1024), f32),
            vmem((2, 8, B, B), f32), vmem((2, 3, 8, 32, B), f32),
            vmem((4, 8, 64, H), f32), vmem((2048, H), bf16), vmem((2048, H), bf16),
            vmem((B, 17 * B), f32), vmem((15, 8, 17 * B), f32), vmem((B, B), f32), vmem((8, 17 * B), f32),
            dma, dma, dma((2,)), dma((2,)), dma((2,)), dma((2,)), dma((2,)), dma((2,)), dma((2,)), dma((2,)), dma((2,)), dma((2, 4)),
            dma((2,)), dma((2,)), dma((2,)), dma((2, 3)), dma((2,)), dma((2,)), dma, dma((3,)),
            dma((3,)), dma((2,)), dma((3,)), dma((3,)), dma((3, 2)), dma((3, 15)), dma((3,)), dma((3,)),
        ],
        compiler_params=pltpu.CompilerParams(
            collective_id=0, has_side_effects=True, vmem_limit_bytes=63 * 1024 * 1024
        ),
    )(wavefunction, start_block)


def back_kernel(scale, q_ref, out_ref, mid, buf, s1, r1, s2, r2):
    row, col, layer = (lax.axis_index(n) for n in ("row", "col", "layer"))
    turns = [(lax.rem(row + n, 4), lax.rem(row + 4 - n, 4)) for n in range(1, 4)]
    sides = [(lax.rem(col + n, 4), lax.rem(col + 4 - n, 4)) for n in range(1, 4)]
    greet([(to, col, layer) for to, _ in turns] + [(row, to, layer) for to, _ in sides])
    sends = []
    for n, (to, _) in enumerate(turns):
        sends.append(send(q_ref.at[:, band(to, 512)], mid.at[n], s1.at[n], r1.at[n], (to, col, layer)))

    def pass_on(n, src, to):
        @pl.when(to == col)
        def _():
            buf[col] = src[...]

        @pl.when(to != col)
        def _():
            send(src, buf.at[col], s2.at[n], r2.at[lax.rem(to + 4 - col, 4) - 1], (row, to, layer))

    pass_on(0, q_ref.at[:, band(row, 512)], row)
    for n, (_, source) in enumerate(turns):
        done(mid.at[n], r1.at[n])
        pass_on(n + 1, mid.at[n], source)
    for n, (_, source) in enumerate(sides):
        done(buf.at[source], r2.at[n])
    for n in range(4):
        out_ref[n * 32 : (n + 1) * 32, :] = buf[n] * scale
    for s in sends:
        s.wait_send()
    for n, to in enumerate([row] + [source for _, source in turns]):

        @pl.when(to != col)
        def _():
            done(buf.at[0], s2.at[n])


def back(q, scale):
    dma = pltpu.SemaphoreType.DMA
    return pl.pallas_call(
        lambda *refs: back_kernel(scale, *refs),
        out_shape=jax.ShapeDtypeStruct((B, 512), f32),
        in_specs=[pl.BlockSpec(memory_space=pltpu.VMEM)],
        out_specs=pl.BlockSpec(memory_space=pltpu.VMEM),
        scratch_shapes=[
            pltpu.VMEM((3, 32, 512), f32), pltpu.VMEM((4, 32, 512), f32), dma((3,)), dma((3,)), dma((4,)), dma((3,)),
        ],
        compiler_params=pltpu.CompilerParams(collective_id=1, has_side_effects=True),
    )(q)


def factor(d_ref, y_ref, fill):
    lane = lax.broadcasted_iota(jnp.int32, (8, B), 1)
    sub = lax.broadcasted_iota(jnp.int32, (8, B), 0)
    full = lambda x: jnp.broadcast_to(x, (8, B))
    state = [d_ref[8 * i : 8 * i + 8, :] for i in range(16)]
    for b in range(8):
        base = 16 * b
        near = [[full(state[i][:, base + j : base + j + 1]) for i in range(2 * b, 2 * b + 2)] for j in range(16)]
        far = [[full(state[i][:, base + j : base + j + 1]) for i in range(2 * b + 2, 16)] for j in range(16)]
        turned = [near[j] + far[j] for j in range(16)]
        c = [[jnp.where(sub < 8, turned[j][h], 0.0) for h in range(2)] for j in range(16)]
        inside = (lane >= base) & (lane < base + 16)
        v = [jnp.where(inside, jnp.where(lane - base - 8 * h == sub, 1.0, 0.0), state[2 * b + h]) for h in range(2)]
        out, pivots, inverse = list(v), [c[0][0], c[8][1]], [1.0, 1.0]
        for j in range(16):
            h, s = divmod(j, 8)
            q = 1.0 / c[j][h]
            r = full(q[s : s + 1, :])
            out[h] = jnp.where(sub >= s, v[h], out[h])
            pivots[h] = jnp.where(sub >= s, c[j][h], pivots[h])
            inverse[h] = jnp.where(sub >= s, q, inverse[h])
            f = [c[j][g] * r for g in range(2)]
            f[h] = jnp.where(sub == s, 0.0, f[h])
            t = full(v[h][s : s + 1, :])
            v = [v[g] - f[g] * t for g in range(2)]
            for k in range(j + 1, 16):
                t = full(c[k][h][s : s + 1, :])
                c[k] = [c[k][g] - f[g] * t for g in range(2)]
        w = []
        for h in range(2):
            y_ref[base + 8 * h : base + 8 * h + 8, :] = jnp.where(lane <= base + 8 * h + sub, out[h] * lax.rsqrt(pivots[h]), 0.0)
            x = v[h] * inverse[h]
            w += [full(x[j : j + 1, :]) for j in range(8)]
        for i in range(2 * b + 2, 16):
            p = [turned[j][i - 2 * b] * w[j] for j in range(16)]
            while len(p) > 1:
                p = [p[k] + p[k + 1] for k in range(0, len(p), 2)]
            state[i] = jnp.where(inside, 0.0, state[i]) - p[0]
        fill(2 * b)
        fill(2 * b + 1)


def solve_kernel(plan, g_ref, s_ref, q_ref, w, lhi, llo, yhi, ylo, d, y, sems):
    sizes = [((l + 1) * B, (16 - l) * B) for l in range(8)]

    def strip(s, first, n):
        l = min(s, 15 - s)

        @pl.loop(0, 16)
        def _(q):
            rows = pl.ds(pl.multiple_of(s * B + q * 8, 8), 8)
            pltpu.make_async_copy(g_ref.at[q, l, :, first : first + n], w.at[rows, 0:n], sems.at[s]).start()

    for l, (n, m) in enumerate(sizes):
        strip(l, 0, n)
    for l, (n, m) in reversed(list(enumerate(sizes))):
        strip(15 - l, n, m)

    slab = slice(16 * B, 16 * B + 32)
    w[slab, :] = s_ref[...]
    w[0:B, 7 * H : 8 * H] = jnp.zeros((B, H), f32)

    @pl.loop(0, 10)
    def _(i):
        for part in (lhi, llo):
            part[band(i, H), 0:H] = jnp.zeros((H, H), bf16)

    @pl.loop(1, 8)
    def _(i):
        for part in (lhi, llo):
            part[18 * B : 20 * B, band(i, H)] = jnp.zeros((H, H), bf16)
            part[14 * B : 16 * B, band(i, H)] = jnp.zeros((H, H), bf16)

    yhi[0:B, B:H] = jnp.zeros((B, B), bf16)
    ylo[0:B, B:H] = jnp.zeros((B, B), bf16)
    for l in range(2):
        done(w.at[l * B : (l + 1) * B, 0 : (l + 1) * B], sems.at[l])

    def nt3(a, b):
        (ahi, alo), (bhi, blo) = a, b
        return nt(ahi, bhi) + nt(ahi, blo) + nt(alo, bhi)

    def nn3(a, b):
        (ahi, alo), (bhi, blo) = a, b
        return nn(ahi, bhi) + nn(ahi, blo) + nn(alo, bhi)

    def held(rows, cols):
        return lhi[rows, cols], llo[rows, cols]

    def panel(rows, cols):
        p = nt3(split(w[rows, cols]), (yhi[...], ylo[...]))
        lhi[rows, cols], llo[rows, cols] = split(p)
        return p

    @pl.loop(0, 8)
    def _(K):
        c0 = pl.ds(pl.multiple_of(K * H, H), B)
        c1 = pl.ds(pl.multiple_of(K * H + B, B), B)
        both = band(K, H)
        def half(t):
            code = plan[K * 32 + t]
            i, J, source = lax.div(code, 256), lax.rem(lax.div(code, 16), 16), lax.rem(code, 16)
            rows, cols, old = band(lax.rem(i, 18), B), band(J, H), band(source, H)
            w[rows, cols] -= nt3(held(band(i, B), old), held(cols, old))

        def rows_of(b):
            J = K + b
            real = (J < 8) & (K > 0)
            cols = band(jnp.where(real, J, 7), H)
            source = pl.ds(pl.multiple_of(jnp.where(real, 16 * B, 18 * B), B), 32)
            old = band(jnp.maximum(K - 1, 0), H)
            w[slab, cols] -= nt3(held(source, old), held(cols, old))

        def fill(b):
            half(b)
            if b < 8:
                rows_of(b)

        d[...] = w[c0, c0]
        factor(d, y, fill)
        first = split(y[...])
        yhi[0:B, 0:B], ylo[0:B, 0:B] = first
        l21 = split(nt3(split(w[c1, c0]), first))
        d[...] = w[c1, c1] - nt3(l21, l21)
        corner = split(nn3(l21, first))
        factor(d, y, lambda b: half(16 + b))
        second = split(y[...])
        yhi[B:H, B:H], ylo[B:H, B:H] = second
        yhi[B:H, 0:B], ylo[B:H, 0:B] = split(-nn3(second, corner))

        @pl.when(K == 0)
        def _():
            for l in range(2, 16):
                done(w.at[l * B : (l + 1) * B, 0 : (l + 1) * B], sems.at[l])

        q_ref[:, both] = panel(slab, both)

        @pl.loop(K + 1, 8)
        def _(I):
            panel(band(I, H), both)

        @pl.when(K < 7)
        def _():
            rows = band(K + 1, H)
            w[rows, rows] -= nt3(held(rows, both), held(rows, both))


def schedule():
    plan, waiting = [], []
    blank = 18 * 256 + 7 * 16
    for K in range(8):
        if K:
            waiting += [
                (J, K - 1, i) for J in range(K, 8) for i in range(2 * J, 16) if not (J == K and i < 2 * J + 2)
            ]
        waiting.sort()
        now, waiting = waiting[:32], waiting[32:]
        assert all(J > K + 1 or (J > K and i >= 2 * J + 2) for J, _, i in waiting)
        plan += [i * 256 + J * 16 + source for J, source, i in now] + [blank] * (32 - len(now))
    return jnp.array(plan, jnp.int32)


def solve(gram, slab):
    return pl.pallas_call(
        solve_kernel,
        out_shape=jax.ShapeDtypeStruct((32, 2048), f32),
        in_specs=[
            pl.BlockSpec(memory_space=pltpu.SMEM), pl.BlockSpec(memory_space=pl.ANY), pl.BlockSpec(memory_space=pltpu.VMEM),
        ],
        out_specs=pl.BlockSpec(memory_space=pltpu.VMEM),
        scratch_shapes=[
            pltpu.VMEM((16 * B + 32, 2048), f32), pltpu.VMEM((2560, 2048), bf16), pltpu.VMEM((2560, 2048), bf16),
            pltpu.VMEM((H, H), bf16), pltpu.VMEM((H, H), bf16),
            pltpu.VMEM((B, B), f32), pltpu.VMEM((B, B), f32), pltpu.SemaphoreType.DMA((16,)),
        ],
        compiler_params=pltpu.CompilerParams(vmem_limit_bytes=60 * 1024 * 1024),
    )(schedule(), gram, slab)


def shards(wavefunction, start_block):
    gram, slab = front(wavefunction, start_block)
    gram = gram.reshape(16, 8, 8, 17 * B)
    return back(solve(gram, slab), math.sqrt(4096.0))


def solution(mesh):
    placed = (P("row", "col"), P(("col", "layer"), "row"))
    return jax.shard_map(
        shards, mesh=mesh, in_specs=placed, out_specs=P(("col", "layer"), "row"), check_vma=False
    )
```
